32 devices in a mesh: tm: 4 (over y, core), space: 8 (over z, x).
Axes of the slice: x: 2, y: 2, z: 4, core: 2. Of those that a mesh axis runs over, the one named last changes fastest.
Arguments:
- observed: float32 [8, 48, 1440], P('tm', 'space'), may hold values from -8 to 8
- noise_var: float32 [8], replicated, may hold values from 0.05 to 1
- spectral_var: float32 [1440, 48], P('space'), may hold values from 0.2 to 5
- time_scale: float32 [1440, 48], P('space'), may hold values from 1.5 to 2
Outputs:
- smoothed: float32 [8, 48, 1440], P('tm', 'space')
The draws below stay inside these ranges and needn't reach their ends.
All inputs are finite; a program needn't handle non-finite values.
Results may differ from the reference program's by a relative error of at most 0.00007.
Values sent between devices are 32-bit elements; how exact they have to be, the bound alone decides.
A program may use at most 64 MiB of HBM per device.

```python
import math
import jax
import jax.numpy as jnp
from jax import lax

LON = 1440
LAT = 48
HOURS = 8


def level_of(rng, shape, pieces, least, high):
    def one(axis_at, shards_of):
        heights = jax.random.uniform(jax.random.fold_in(jax.random.fold_in(rng, 6), axis_at), (shards_of,), jnp.float32, least / len(pieces), high / len(pieces))
        return jnp.repeat(jnp.exp(heights), shape[axis_at] // shards_of).reshape((-1,) + (1,) * (len(shape) - axis_at - 1))

    gain = one(*pieces[0])
    for cut in pieces[1:]:
        gain = gain * one(*cut)
    return gain


def centred(key, extent, spread, bound, pieces=(), dtype=jnp.bfloat16):
    drawn = jax.random.normal(key, extent, jnp.float32) * spread
    if len(pieces) > 0:
        drawn = level_of(key, extent, pieces, -0.22, 0.18) * drawn
    return jnp.clip(drawn, min=-bound, max=bound).astype(dtype)


def setup_inputs(seed: int = 0) -> dict:
    arg_keys = jax.random.split(jax.random.key(seed), 5)
    return {
        "observed": centred(arg_keys[0], (HOURS, LAT, LON), 1.5, 8.0, ((0, 4), (1, 8)), jnp.float32),
        "noise_var": jnp.clip(jnp.exp(jax.random.uniform(arg_keys[1], (HOURS,), jnp.float32, math.log(0.05), math.log(1.0))), 0.05, 1.0),
        "spectral_var": jnp.clip(jnp.exp(math.log(5.0) - 3.218876 * jax.random.uniform(arg_keys[2], (LON, LAT), jnp.float32) ** level_of(arg_keys[2], (LON, LAT), ((0, 8),), -0.2, 0.2)), 0.2, 5.0),
        "time_scale": jnp.clip(jnp.exp(math.log(2.0) - 0.2876821 * jax.random.uniform(arg_keys[3], (LON, LAT), jnp.float32) ** level_of(arg_keys[3], (LON, LAT), ((0, 8),), -0.2, 0.2)), 1.5, 2.0),
    }


HIGHEST = lax.Precision.HIGHEST
ROOT_FIVE = 2.23606797749979
NILPOTENT = ((1.0, 1.0, 0.0), (0.0, 1.0, 1.0), (-1.0, -3.0, -2.0))
NILPOTENT_SQUARED = ((1.0, 2.0, 1.0), (-1.0, -2.0, -1.0), (1.0, 2.0, 1.0))
STATIONARY = ((1.0, 0.0, -1.0 / 3.0), (0.0, 1.0 / 3.0, 0.0), (-1.0 / 3.0, 0.0, 1.0))

def lon_basis(size):
    mode_index = lax.broadcasted_iota(jnp.int32, (size, size), 0)
    longitude = lax.broadcasted_iota(jnp.int32, (size, size), 1)
    half_size = size // 2
    sine_rows = mode_index > half_size
    frequency = jnp.where(sine_rows, mode_index - half_size, mode_index)
    radians = (frequency * longitude % size).astype(jnp.float32) * (2.0 * math.pi / size)
    waveform = jnp.where(sine_rows, jnp.sin(radians), jnp.cos(radians))
    edge_rows = (mode_index == 0) | (mode_index == half_size)
    weight = jnp.where(edge_rows, math.sqrt(1.0 / size), math.sqrt(2.0 / size))
    return waveform * weight

def lat_basis(size):
    wavenumber = lax.broadcasted_iota(jnp.int32, (size, size), 0)
    latitude = lax.broadcasted_iota(jnp.int32, (size, size), 1)
    radians = (wavenumber * (2 * latitude + 1) % (4 * size)).astype(jnp.float32) * (math.pi / (2.0 * size))
    weight = jnp.where(wavenumber == 0, math.sqrt(1.0 / size), math.sqrt(2.0 / size))
    return jnp.cos(radians) * weight

def mat_mul(left, right):
    return [[left[across][0] * right[0][within] + left[across][1] * right[1][within] + left[across][2] * right[2][within] for within in range(3)] for across in range(3)]

def mat_vec(matrix, vector):
    return [matrix[across][0] * vector[0] + matrix[across][1] * vector[1] + matrix[across][2] * vector[2] for across in range(3)]

def transposed(matrix):
    return [[matrix[within][across] for within in range(3)] for across in range(3)]

def inverted(matrix):
    cofactor = [[matrix[1][1] * matrix[2][2] - matrix[1][2] * matrix[2][1], matrix[0][2] * matrix[2][1] - matrix[0][1] * matrix[2][2], matrix[0][1] * matrix[1][2] - matrix[0][2] * matrix[1][1]], [matrix[1][2] * matrix[2][0] - matrix[1][0] * matrix[2][2], matrix[0][0] * matrix[2][2] - matrix[0][2] * matrix[2][0], matrix[0][2] * matrix[1][0] - matrix[0][0] * matrix[1][2]], [matrix[1][0] * matrix[2][1] - matrix[1][1] * matrix[2][0], matrix[0][1] * matrix[2][0] - matrix[0][0] * matrix[2][1], matrix[0][0] * matrix[1][1] - matrix[0][1] * matrix[1][0]]]
    determinant = matrix[0][0] * cofactor[0][0] + matrix[0][1] * cofactor[1][0] + matrix[0][2] * cofactor[2][0]
    return [[cofactor[across][within] / determinant for within in range(3)] for across in range(3)]

def model_terms(variance, scale):
    decay_rate = ROOT_FIVE / scale
    damping = jnp.exp(-decay_rate)
    transition = [[damping * ((1.0 if across == within else 0.0) + decay_rate * NILPOTENT[across][within] + 0.5 * decay_rate * decay_rate * NILPOTENT_SQUARED[across][within]) for within in range(3)] for across in range(3)]
    stationary = [[variance * STATIONARY[across][within] for within in range(3)] for across in range(3)]
    carried = mat_mul(mat_mul(transition, stationary), transposed(transition))
    process_noise = [[stationary[across][within] - carried[across][within] for within in range(3)] for across in range(3)]
    return (transition, stationary, process_noise)

def predict_cov(covariance, transition, process_noise):
    carried = mat_mul(mat_mul(transition, covariance), transposed(transition))
    return [[carried[across][within] + process_noise[across][within] for within in range(3)] for across in range(3)]

def gain_and_cov(predicted_cov, noise):
    innovation_var = predicted_cov[0][0] + noise
    kalman_gain = [predicted_cov[across][0] / innovation_var for across in range(3)]
    covariance = [[predicted_cov[across][within] - kalman_gain[across] * predicted_cov[0][within] for within in range(3)] for across in range(3)]
    return (kalman_gain, covariance)

def smooth_series(spectra, noise_var, variance, scale):
    transition, stationary, process_noise = model_terms(variance, scale)
    zeros = jnp.zeros_like(variance)

    def forward(carry, inputs):
        mean_state, covariance = carry
        observed, noise = inputs
        predicted_cov = predict_cov(covariance, transition, process_noise)
        smoother_gain = mat_mul(mat_mul(covariance, transposed(transition)), inverted(predicted_cov))
        predicted = mat_vec(transition, mean_state)
        kalman_gain, covariance = gain_and_cov(predicted_cov, noise)
        residual = observed - predicted[0]
        mean_state = [predicted[across] + kalman_gain[across] * residual for across in range(3)]
        return ((mean_state, covariance), (mean_state, smoother_gain))
    _, (means, gains) = lax.scan(forward, ([zeros, zeros, zeros], stationary), (spectra, noise_var))

    def backward(later, inputs):
        mean_state, smoother_gain = inputs
        projected = mat_vec(transition, mean_state)
        difference = [later[across] - projected[across] for across in range(3)]
        correction = mat_vec(smoother_gain, difference)
        smoothed_state = [mean_state[across] + correction[across] for across in range(3)]
        return (smoothed_state, smoothed_state[0])
    last_state = [means[across][-1] for across in range(3)]
    earlier_means = [means[across][:-1] for across in range(3)]
    next_gains = [[gains[across][within][1:] for within in range(3)] for across in range(3)]
    _, field = lax.scan(backward, last_state, (earlier_means, next_gains), reverse=True)
    return jnp.concatenate([field, last_state[0][None]], axis=0)

def reference(observed, noise_var, spectral_var, time_scale):
    lon_table = lon_basis(LON)
    lat_table = lat_basis(LAT)
    spectra = jnp.einsum('hal,jl->hja', observed, lon_table, precision=HIGHEST)
    spectra = jnp.einsum('hja,na->hjn', spectra, lat_table, precision=HIGHEST)
    blocks = 16
    shaped = spectra.reshape(HOURS, blocks, LON // blocks, LAT).transpose(1, 0, 2, 3)
    variances = spectral_var.reshape(blocks, LON // blocks, LAT)
    scales = time_scale.reshape(blocks, LON // blocks, LAT)

    def per_block(bundle):
        series, variance, scale = bundle
        return smooth_series(series, noise_var, variance, scale)
    smooth = lax.map(per_block, (shaped, variances, scales))
    smooth = smooth.transpose(1, 0, 2, 3).reshape(HOURS, LON, LAT)
    latitude_grid = jnp.einsum('hjn,na->hja', smooth, lat_table, precision=HIGHEST)
    return jnp.einsum('hja,jl->hal', latitude_grid, lon_table, precision=HIGHEST)
```

```python
import functools
import math

import jax
import jax.numpy as jnp
import numpy as np
from jax import lax
from jax.experimental import pallas as pl
from jax.experimental.pallas import tpu as pltpu
from jax.sharding import PartitionSpec as P

HIGHEST = lax.Precision.HIGHEST
ROOT_FIVE = 2.23606797749979
NILPOTENT = ((1.0, 1.0, 0.0), (0.0, 1.0, 1.0), (-1.0, -3.0, -2.0))
NILPOTENT_SQUARED = ((1.0, 2.0, 1.0), (-1.0, -2.0, -1.0), (1.0, 2.0, 1.0))
STATIONARY = ((1.0, 0.0, -1.0 / 3.0), (0.0, 1.0 / 3.0, 0.0), (-1.0 / 3.0, 0.0, 1.0))


def lon_basis(size):
    mode_index = lax.broadcasted_iota(jnp.int32, (size, size), 0)
    longitude = lax.broadcasted_iota(jnp.int32, (size, size), 1)
    half_size = size // 2
    sine_rows = mode_index > half_size
    frequency = jnp.where(sine_rows, mode_index - half_size, mode_index)
    radians = (frequency * longitude % size).astype(jnp.float32) * (2.0 * math.pi / size)
    waveform = jnp.where(sine_rows, jnp.sin(radians), jnp.cos(radians))
    edge_rows = (mode_index == 0) | (mode_index == half_size)
    weight = jnp.where(edge_rows, math.sqrt(1.0 / size), math.sqrt(2.0 / size))
    return waveform * weight


def lat_basis(size):
    wavenumber = lax.broadcasted_iota(jnp.int32, (size, size), 0)
    latitude = lax.broadcasted_iota(jnp.int32, (size, size), 1)
    radians = (wavenumber * (2 * latitude + 1) % (4 * size)).astype(jnp.float32) * (
        math.pi / (2.0 * size)
    )
    weight = jnp.where(wavenumber == 0, math.sqrt(1.0 / size), math.sqrt(2.0 / size))
    return jnp.cos(radians) * weight


def mat_mul(left, right):
    return [
        [
            left[across][0] * right[0][within]
            + left[across][1] * right[1][within]
            + left[across][2] * right[2][within]
            for within in range(3)
        ]
        for across in range(3)
    ]


def mat_vec(matrix, vector):
    return [
        matrix[across][0] * vector[0]
        + matrix[across][1] * vector[1]
        + matrix[across][2] * vector[2]
        for across in range(3)
    ]


def transposed(matrix):
    return [[matrix[within][across] for within in range(3)] for across in range(3)]


def inverted(matrix):
    cofactor = [
        [
            matrix[1][1] * matrix[2][2] - matrix[1][2] * matrix[2][1],
            matrix[0][2] * matrix[2][1] - matrix[0][1] * matrix[2][2],
            matrix[0][1] * matrix[1][2] - matrix[0][2] * matrix[1][1],
        ],
        [
            matrix[1][2] * matrix[2][0] - matrix[1][0] * matrix[2][2],
            matrix[0][0] * matrix[2][2] - matrix[0][2] * matrix[2][0],
            matrix[0][2] * matrix[1][0] - matrix[0][0] * matrix[1][2],
        ],
        [
            matrix[1][0] * matrix[2][1] - matrix[1][1] * matrix[2][0],
            matrix[0][1] * matrix[2][0] - matrix[0][0] * matrix[2][1],
            matrix[0][0] * matrix[1][1] - matrix[0][1] * matrix[1][0],
        ],
    ]
    determinant = (
        matrix[0][0] * cofactor[0][0]
        + matrix[0][1] * cofactor[1][0]
        + matrix[0][2] * cofactor[2][0]
    )
    return [[cofactor[across][within] / determinant for within in range(3)] for across in range(3)]


def model_terms(variance, scale):
    decay_rate = ROOT_FIVE / scale
    damping = jnp.exp(-decay_rate)
    transition = [
        [
            damping
            * (
                (1.0 if across == within else 0.0)
                + decay_rate * NILPOTENT[across][within]
                + 0.5 * decay_rate * decay_rate * NILPOTENT_SQUARED[across][within]
            )
            for within in range(3)
        ]
        for across in range(3)
    ]
    stationary = [
        [variance * STATIONARY[across][within] for within in range(3)] for across in range(3)
    ]
    carried = mat_mul(mat_mul(transition, stationary), transposed(transition))
    process_noise = [
        [stationary[across][within] - carried[across][within] for within in range(3)]
        for across in range(3)
    ]
    return (transition, stationary, process_noise)


def predict_cov(covariance, transition, process_noise):
    carried = mat_mul(mat_mul(transition, covariance), transposed(transition))
    return [
        [carried[across][within] + process_noise[across][within] for within in range(3)]
        for across in range(3)
    ]


def gain_and_cov(predicted_cov, noise):
    innovation_var = predicted_cov[0][0] + noise
    kalman_gain = [predicted_cov[across][0] / innovation_var for across in range(3)]
    covariance = [
        [
            predicted_cov[across][within] - kalman_gain[across] * predicted_cov[0][within]
            for within in range(3)
        ]
        for across in range(3)
    ]
    return (kalman_gain, covariance)


def smooth_series(spectra, noise_var, variance, scale):
    transition, stationary, process_noise = model_terms(variance, scale)
    zeros = jnp.zeros_like(variance)

    def forward(carry, inputs):
        mean_state, covariance = carry
        observed, noise = inputs
        predicted_cov = predict_cov(covariance, transition, process_noise)
        smoother_gain = mat_mul(
            mat_mul(covariance, transposed(transition)), inverted(predicted_cov)
        )
        predicted = mat_vec(transition, mean_state)
        kalman_gain, covariance = gain_and_cov(predicted_cov, noise)
        residual = observed - predicted[0]
        mean_state = [predicted[across] + kalman_gain[across] * residual for across in range(3)]
        return ((mean_state, covariance), (mean_state, smoother_gain))

    _, (means, gains) = lax.scan(forward, ([zeros, zeros, zeros], stationary), (spectra, noise_var))

    def backward(later, inputs):
        mean_state, smoother_gain = inputs
        projected = mat_vec(transition, mean_state)
        difference = [later[across] - projected[across] for across in range(3)]
        correction = mat_vec(smoother_gain, difference)
        smoothed_state = [mean_state[across] + correction[across] for across in range(3)]
        return (smoothed_state, smoothed_state[0])

    last_state = [means[across][-1] for across in range(3)]
    earlier_means = [means[across][:-1] for across in range(3)]
    next_gains = [[gains[across][within][1:] for within in range(3)] for across in range(3)]
    _, field = lax.scan(backward, last_state, (earlier_means, next_gains), reverse=True)
    return jnp.concatenate([field, last_state[0][None]], axis=0)


def per_device_general(observed, noise_var, spectral_var, time_scale):
    hours_dev, lat_dev, lon_size = observed.shape
    band_count = lax.axis_size("space")
    lat_size = lat_dev * band_count
    modes_dev = lon_size // band_count
    lon_table = lon_basis(lon_size)
    lat_table = lat_basis(lat_size).reshape(lat_size, band_count, lat_dev)
    grid_rows = observed.reshape(hours_dev * lat_dev, lon_size)
    spectra = lax.dot_general(lon_table, grid_rows, (((1,), (1,)), ((), ())), precision=HIGHEST)
    by_mode = lax.all_to_all(spectra, "space", split_axis=0, concat_axis=1, tiled=True)
    by_mode = by_mode.reshape(modes_dev, band_count, hours_dev, lat_dev)
    coefficients = jnp.einsum("msha,nsa->hmn", by_mode, lat_table, precision=HIGHEST)
    flat = coefficients.reshape(hours_dev, modes_dev * lat_size)
    hourly = lax.all_to_all(flat, "tm", split_axis=1, concat_axis=0, tiled=True)
    share = flat.shape[1] // lax.axis_size("tm")
    offset = lax.axis_index("tm") * share
    variance = lax.dynamic_slice_in_dim(spectral_var.reshape(-1), offset, share)
    scale = lax.dynamic_slice_in_dim(time_scale.reshape(-1), offset, share)
    series = smooth_series(hourly, noise_var, variance, scale)
    smooth = lax.all_to_all(series, "tm", split_axis=0, concat_axis=1, tiled=True).reshape(
        hours_dev, modes_dev, lat_size
    )
    latitude_grid = jnp.einsum("hmn,nsa->msha", smooth, lat_table, precision=HIGHEST)
    latitude_grid = latitude_grid.reshape(modes_dev, band_count * hours_dev * lat_dev)
    by_band = lax.all_to_all(latitude_grid, "space", split_axis=1, concat_axis=0, tiled=True)
    field = lax.dot_general(by_band, lon_table, (((0,), (0,)), ((), ())), precision=HIGHEST)
    return field.reshape(hours_dev, lat_dev, lon_size)


LANES = 128
ROWS = 8
MESH = pl.DeviceIdType.MESH
NT = (((1,), (1,)), ((), ()))
NN = (((1,), (0,)), ((), ()))


def round_up(value, unit):
    return -(-value // unit) * unit


def lon_tables(lon_size, times, bands, slots_used):
    half = lon_size // 2
    modes_dev = lon_size // bands
    slots = modes_dev // times
    mode = (
        np.arange(bands)[None, :, None] * modes_dev
        + np.arange(times)[:, None, None]
        + times * np.arange(slots)[None, None, :]
    )
    sine = mode > half
    frequency = np.where(sine, mode - half, mode)
    radians = (frequency[..., None] * np.arange(half) % lon_size) * (2.0 * math.pi / lon_size)
    waveform = np.where(sine[..., None], np.sin(radians), np.cos(radians))
    edge = (mode == 0) | (mode == half)
    table = waveform * np.where(edge, math.sqrt(1.0 / lon_size), math.sqrt(2.0 / lon_size))[..., None]
    full = np.zeros((times, bands, slots_used, round_up(half, LANES)), np.float32)
    full[:, :, :slots, :half] = table
    high = full.astype(jnp.bfloat16)
    low = (full - high.astype(np.float32)).astype(jnp.bfloat16)
    return high, low


def lat_tables(lat_size, bands):
    lat_dev = lat_size // bands
    wavenumber = np.arange(lat_size)[:, None]
    latitude = np.arange(lat_size)[None, :]
    radians = (wavenumber * (2 * latitude + 1) % (4 * lat_size)) * (math.pi / (2.0 * lat_size))
    table = np.cos(radians) * np.where(wavenumber == 0, math.sqrt(1.0 / lat_size), math.sqrt(2.0 / lat_size))
    full = np.zeros((lat_size, bands, ROWS), np.float32)
    full[:, :, :lat_dev] = table.reshape(lat_size, bands, lat_dev)
    full = full.reshape(lat_size, bands * ROWS)
    return full, np.ascontiguousarray(full.T)


def split(value):
    high = value.astype(jnp.bfloat16)
    low = (value - high.astype(jnp.float32)).astype(jnp.bfloat16)
    return high, low


def swap_halves(first, second):
    left = lax.broadcasted_iota(jnp.int32, first.shape, 1) < LANES // 2
    return (
        jnp.where(left, first, pltpu.roll(second, LANES // 2, 1)),
        jnp.where(left, pltpu.roll(first, LANES // 2, 1), second),
    )


def symmetric_gains(noise_ref, variance, scale, transition_ref, gain_ref, smoother_ref):
    hours = gain_ref.shape[0]
    transition, stationary, process = model_terms(variance, scale)
    pairs = [(0, 0), (0, 1), (0, 2), (1, 1), (1, 2), (2, 2)]
    for row in range(3):
        for column in range(3):
            transition_ref[row, column] = transition[row][column]

    def unpack(packed):
        matrix = [[None] * 3 for _ in range(3)]
        for (row, column), value in zip(pairs, packed):
            matrix[row][column] = matrix[column][row] = value
        return matrix

    def update(predicted, hour):
        inverse_var = 1.0 / (predicted[0][0] + noise_ref[hour])
        gain = [predicted[row][0] * inverse_var for row in range(3)]
        for row in range(3):
            gain_ref[hour, row] = gain[row]
        return [predicted[row][column] - gain[row] * predicted[0][column] for row, column in pairs]

    def step(hour, packed):
        covariance = unpack(packed)
        moved = mat_mul(transition, covariance)
        predicted = unpack(
            [
                moved[row][0] * transition[column][0]
                + moved[row][1] * transition[column][1]
                + moved[row][2] * transition[column][2]
                + process[row][column]
                for row, column in pairs
            ]
        )
        c00 = predicted[1][1] * predicted[2][2] - predicted[1][2] * predicted[1][2]
        c01 = predicted[0][2] * predicted[1][2] - predicted[0][1] * predicted[2][2]
        c02 = predicted[0][1] * predicted[1][2] - predicted[0][2] * predicted[1][1]
        c11 = predicted[0][0] * predicted[2][2] - predicted[0][2] * predicted[0][2]
        c12 = predicted[0][1] * predicted[0][2] - predicted[0][0] * predicted[1][2]
        c22 = predicted[0][0] * predicted[1][1] - predicted[0][1] * predicted[0][1]
        inverse_det = 1.0 / (predicted[0][0] * c00 + predicted[0][1] * c01 + predicted[0][2] * c02)
        cofactors = unpack([c00, c01, c02, c11, c12, c22])
        for row in range(3):
            scaled = [moved[within][row] * inverse_det for within in range(3)]
            for column in range(3):
                smoother_ref[hour - 1, row, column] = (
                    scaled[0] * cofactors[0][column]
                    + scaled[1] * cofactors[1][column]
                    + scaled[2] * cofactors[2][column]
                )
        return tuple(update(predicted, hour))

    first = tuple(update(stationary, 0))
    lax.fori_loop(1, hours, step, first)


def smoother_kernel(
    times,
    bands,
    slots_used,
    observed_ref,
    noise_ref,
    variance_ref,
    scale_ref,
    forward_lat_ref,
    inverse_lat_ref,
    high_hbm,
    low_hbm,
    out_ref,
    high,
    low,
    folded,
    outbox,
    inbox,
    outbox_back,
    inbox_back,
    transition_ref,
    gain_ref,
    smoother_ref,
    table_sem,
    send_sem,
    recv_sem,
    send_back_sem,
    recv_back_sem,
):
    devices = times * bands
    my_time = lax.axis_index("tm")
    my_band = lax.axis_index("space")
    me = my_time * bands + my_band
    lat_dev, lon_size = observed_ref.shape[1], observed_ref.shape[2]
    half = lon_size // 2
    hours = gain_ref.shape[0]
    n_half = gain_ref.shape[2]
    width = LANES // 2

    def table_copy(time, which):
        source, target = ((high_hbm, high), (low_hbm, low))[which]
        return pltpu.make_async_copy(
            source.at[time], target.at[time, :, pl.ds(0, slots_used), :], table_sem.at[time, which]
        )

    for time in range(times):
        table_copy(time, 0).start()
        table_copy(time, 1).start()

    inbox[...] = jnp.zeros_like(inbox)
    inbox_back[...] = jnp.zeros_like(inbox_back)

    barrier = pltpu.get_barrier_semaphore()

    def greet(step, carry):
        peer = lax.rem(me + step, devices)
        pl.semaphore_signal(
            barrier, inc=1, device_id=(peer // bands, lax.rem(peer, bands)), device_id_type=MESH
        )
        return carry

    lax.fori_loop(1, devices, greet, 0)

    spare = width - slots_used
    high[:, :, slots_used:, :] = jnp.zeros((times, bands, spare, high.shape[3]), high.dtype)
    low[:, :, slots_used:, :] = jnp.zeros((times, bands, spare, low.shape[3]), low.dtype)
    folded[...] = jnp.zeros_like(folded)
    for hour in range(2):
        early = observed_ref[hour, :, :half]
        late = observed_ref[hour, :, half:]
        folded[0, hour * ROWS : hour * ROWS + lat_dev, :half] = early + late
        folded[1, hour * ROWS : hour * ROWS + lat_dev, :half] = early - late
    rows = []
    for parity in range(2):
        upper, lower = split(folded[parity])
        rows.append((jnp.concatenate([upper, lower], axis=0), upper))

    symmetric_gains(noise_ref, variance_ref[...], scale_ref[...], transition_ref, gain_ref, smoother_ref)

    def flat(ref, time):
        return ref[time].reshape(bands * width, ref.shape[3])

    for time in range(times):
        table_copy(time, 0).wait()
        table_copy(time, 1).wait()
        both, upper = rows[time % 2]
        wide = lax.dot_general(both, flat(high, time), NT, preferred_element_type=jnp.float32)
        rest = lax.dot_general(upper, flat(low, time), NT, preferred_element_type=jnp.float32)
        spectra = wide[: 2 * ROWS] + wide[2 * ROWS :] + rest
        for pair in range(bands // 2):
            block = spectra[:, pair * LANES : (pair + 1) * LANES]
            outbox[time, 2 * pair], outbox[time, 2 * pair + 1] = swap_halves(block[:ROWS], block[ROWS:])

    pl.semaphore_wait(barrier, devices - 1)

    def exchange(box, landing, sends, recvs, peer, slot):
        peer_time, peer_band = peer // bands, lax.rem(peer, bands)
        slot_time, slot_band = slot // bands, lax.rem(slot, bands)
        return pltpu.make_async_remote_copy(
            src_ref=box.at[peer_time, peer_band, pl.ds(0, lat_dev)],
            dst_ref=landing.at[slot_time, slot_band, pl.ds(0, lat_dev)],
            send_sem=sends.at[peer],
            recv_sem=recvs.at[slot],
            device_id=(peer_time, peer_band),
            device_id_type=MESH,
        )

    def send(step, carry):
        peer = lax.rem(me + step, devices)
        exchange(outbox, inbox, send_sem, recv_sem, peer, me).start()
        return carry

    def settle(step, carry):
        peer = lax.rem(me + step, devices)
        exchange(outbox, inbox, send_sem, recv_sem, peer, peer).wait()
        return carry

    lax.fori_loop(1, devices, send, 0)
    inbox[my_time, my_band] = outbox[my_time, my_band]
    lax.fori_loop(1, devices, settle, 0)

    spectra = []
    for time in range(times):
        mixed = lax.dot_general(
            forward_lat_ref[...],
            inbox[time].reshape(bands * ROWS, LANES),
            NN,
            precision=HIGHEST,
            preferred_element_type=jnp.float32,
        )
        spectra.extend(swap_halves(mixed[:n_half], mixed[n_half:]))

    transition = [[transition_ref[row, column] for column in range(3)] for row in range(3)]
    means, predictions = [], [None]
    means.append([gain_ref[0, row] * spectra[0] for row in range(3)])
    for hour in range(1, hours):
        predicted = mat_vec(transition, means[-1])
        residual = spectra[hour] - predicted[0]
        predictions.append(predicted)
        means.append([predicted[row] + gain_ref[hour, row] * residual for row in range(3)])
    smoothed = means[-1]
    series = [None] * hours
    series[hours - 1] = smoothed[0]
    for hour in range(hours - 2, -1, -1):
        difference = [smoothed[row] - predictions[hour + 1][row] for row in range(3)]
        smoothed = [
            means[hour][row]
            + smoother_ref[hour, row, 0] * difference[0]
            + smoother_ref[hour, row, 1] * difference[1]
            + smoother_ref[hour, row, 2] * difference[2]
            for row in range(3)
        ]
        series[hour] = smoothed[0]

    for time in range(times):
        stacked = jnp.concatenate(swap_halves(series[2 * time], series[2 * time + 1]), axis=0)
        grid = lax.dot_general(
            inverse_lat_ref[...], stacked, NN, precision=HIGHEST, preferred_element_type=jnp.float32
        )
        outbox_back[time] = grid.reshape(bands, ROWS, LANES)

    def send_back(step, carry):
        peer = lax.rem(me + step, devices)
        exchange(outbox_back, inbox_back, send_back_sem, recv_back_sem, peer, me).start()
        return carry

    def settle_back(step, carry):
        peer = lax.rem(me + step, devices)
        exchange(outbox_back, inbox_back, send_back_sem, recv_back_sem, peer, peer).wait()
        return carry

    lax.fori_loop(1, devices, send_back, 0)
    inbox_back[my_time, my_band] = outbox_back[my_time, my_band]
    lax.fori_loop(1, devices, settle_back, 0)

    sums = [None, None]
    for time in range(times):
        blocks = []
        for pair in range(bands // 2):
            first, second = swap_halves(inbox_back[time, 2 * pair], inbox_back[time, 2 * pair + 1])
            blocks.append(jnp.concatenate([first, second], axis=0))
        upper, lower = split(jnp.concatenate(blocks, axis=1))
        both = jnp.concatenate([upper, lower], axis=0)
        wide = lax.dot_general(both, flat(high, time), NN, preferred_element_type=jnp.float32)
        rest = lax.dot_general(upper, flat(low, time), NN, preferred_element_type=jnp.float32)
        part = wide[: 2 * ROWS] + wide[2 * ROWS :] + rest
        sums[time % 2] = part if sums[time % 2] is None else sums[time % 2] + part
    early = sums[0] + sums[1]
    late = sums[0] - sums[1]
    for hour in range(2):
        out_ref[hour, :, :half] = early[hour * ROWS : hour * ROWS + lat_dev, :half]
        out_ref[hour, :, half:] = late[hour * ROWS : hour * ROWS + lat_dev, :half]


def per_device_fused(observed, noise_var, spectral_var, time_scale):
    times, bands = lax.axis_size("tm"), lax.axis_size("space")
    hours_dev, lat_dev, lon_size = observed.shape
    hours, lat_size = noise_var.shape[0], spectral_var.shape[1]
    slots = spectral_var.shape[0] // times
    slots_used = round_up(slots, 2 * ROWS)
    n_half, width = lat_size // 2, LANES // 2
    half_padded = round_up(lon_size // 2, LANES)

    def own_modes(array):
        mine = lax.dynamic_index_in_dim(
            array.reshape(slots, times, lat_size), lax.axis_index("tm"), 1, keepdims=False
        )
        mine = jnp.pad(mine.T, ((0, 0), (0, width - slots)), constant_values=1.0)
        return jnp.concatenate([mine[:n_half], mine[n_half:]], axis=1)

    high, low = lon_tables(lon_size, times, bands, slots_used)
    forward_lat, inverse_lat = lat_tables(lat_size, bands)
    in_vmem = pl.BlockSpec(memory_space=pltpu.VMEM)
    in_place = pl.BlockSpec(memory_space=pl.ANY)
    box = pltpu.VMEM((times, bands, ROWS, LANES), jnp.float32)
    table = pltpu.VMEM((times, bands, width, half_padded), jnp.bfloat16)
    dma = pltpu.SemaphoreType.DMA
    return pl.pallas_call(
        functools.partial(smoother_kernel, times, bands, slots_used),
        out_shape=jax.ShapeDtypeStruct(observed.shape, jnp.float32),
        in_specs=[in_vmem, pl.BlockSpec(memory_space=pltpu.SMEM)] + [in_vmem] * 4 + [in_place] * 2,
        out_specs=in_vmem,
        scratch_shapes=[
            table,
            table,
            pltpu.VMEM((2, 2 * ROWS, half_padded), jnp.float32),
            box,
            box,
            box,
            box,
            pltpu.VMEM((3, 3, n_half, LANES), jnp.float32),
            pltpu.VMEM((hours, 3, n_half, LANES), jnp.float32),
            pltpu.VMEM((hours, 3, 3, n_half, LANES), jnp.float32),
            dma((times, 2)),
            dma((times * bands,)),
            dma((times * bands,)),
            dma((times * bands,)),
            dma((times * bands,)),
        ],
        compiler_params=pltpu.CompilerParams(
            collective_id=0, has_side_effects=True, vmem_limit_bytes=48 * 1024 * 1024
        ),
    )(
        observed,
        noise_var,
        own_modes(spectral_var),
        own_modes(time_scale),
        jnp.asarray(forward_lat),
        jnp.asarray(inverse_lat),
        jnp.asarray(high),
        jnp.asarray(low),
    )


def fits(observed, spectral_var):
    times, bands = lax.axis_size("tm"), lax.axis_size("space")
    hours_dev, lat_dev, lon_size = observed.shape
    modes_dev, lat_size = spectral_var.shape
    return (
        hours_dev == 2
        and lat_dev <= ROWS
        and lat_size % (2 * ROWS) == 0
        and bands % 2 == 0
        and times % 2 == 0
        and lon_size % 4 == 0
        and modes_dev % 2 == 0
        and modes_dev % times == 0
        and LANES // 4 < modes_dev // times <= LANES // 2
    )


def per_device(observed, noise_var, spectral_var, time_scale):
    if fits(observed, spectral_var):
        return per_device_fused(observed, noise_var, spectral_var, time_scale)
    return per_device_general(observed, noise_var, spectral_var, time_scale)


def solution(mesh):
    placed = (P("tm", "space", None), P(), P("space", None), P("space", None))
    return jax.shard_map(
        per_device, mesh=mesh, in_specs=placed, out_specs=P("tm", "space", None), check_vma=False
    )
```

```python
import functools
import math

import jax
import jax.numpy as jnp
import numpy as np
from jax import lax
from jax.experimental import pallas as pl
from jax.experimental.pallas import tpu as pltpu
from jax.sharding import PartitionSpec as P

HIGHEST = lax.Precision.HIGHEST
ROOT_FIVE = 2.23606797749979
NILPOTENT = ((1.0, 1.0, 0.0), (0.0, 1.0, 1.0), (-1.0, -3.0, -2.0))
NILPOTENT_SQUARED = ((1.0, 2.0, 1.0), (-1.0, -2.0, -1.0), (1.0, 2.0, 1.0))
STATIONARY = ((1.0, 0.0, -1.0 / 3.0), (0.0, 1.0 / 3.0, 0.0), (-1.0 / 3.0, 0.0, 1.0))


def lon_basis(size):
    mode_index = lax.broadcasted_iota(jnp.int32, (size, size), 0)
    longitude = lax.broadcasted_iota(jnp.int32, (size, size), 1)
    half_size = size // 2
    sine_rows = mode_index > half_size
    frequency = jnp.where(sine_rows, mode_index - half_size, mode_index)
    radians = (frequency * longitude % size).astype(jnp.float32) * (2.0 * math.pi / size)
    waveform = jnp.where(sine_rows, jnp.sin(radians), jnp.cos(radians))
    edge_rows = (mode_index == 0) | (mode_index == half_size)
    weight = jnp.where(edge_rows, math.sqrt(1.0 / size), math.sqrt(2.0 / size))
    return waveform * weight


def lat_basis(size):
    wavenumber = lax.broadcasted_iota(jnp.int32, (size, size), 0)
    latitude = lax.broadcasted_iota(jnp.int32, (size, size), 1)
    radians = (wavenumber * (2 * latitude + 1) % (4 * size)).astype(jnp.float32) * (
        math.pi / (2.0 * size)
    )
    weight = jnp.where(wavenumber == 0, math.sqrt(1.0 / size), math.sqrt(2.0 / size))
    return jnp.cos(radians) * weight


def mat_mul(left, right):
    return [
        [
            left[across][0] * right[0][within]
            + left[across][1] * right[1][within]
            + left[across][2] * right[2][within]
            for within in range(3)
        ]
        for across in range(3)
    ]


def mat_vec(matrix, vector):
    return [
        matrix[across][0] * vector[0]
        + matrix[across][1] * vector[1]
        + matrix[across][2] * vector[2]
        for across in range(3)
    ]


def transposed(matrix):
    return [[matrix[within][across] for within in range(3)] for across in range(3)]


def inverted(matrix):
    cofactor = [
        [
            matrix[1][1] * matrix[2][2] - matrix[1][2] * matrix[2][1],
            matrix[0][2] * matrix[2][1] - matrix[0][1] * matrix[2][2],
            matrix[0][1] * matrix[1][2] - matrix[0][2] * matrix[1][1],
        ],
        [
            matrix[1][2] * matrix[2][0] - matrix[1][0] * matrix[2][2],
            matrix[0][0] * matrix[2][2] - matrix[0][2] * matrix[2][0],
            matrix[0][2] * matrix[1][0] - matrix[0][0] * matrix[1][2],
        ],
        [
            matrix[1][0] * matrix[2][1] - matrix[1][1] * matrix[2][0],
            matrix[0][1] * matrix[2][0] - matrix[0][0] * matrix[2][1],
            matrix[0][0] * matrix[1][1] - matrix[0][1] * matrix[1][0],
        ],
    ]
    determinant = (
        matrix[0][0] * cofactor[0][0]
        + matrix[0][1] * cofactor[1][0]
        + matrix[0][2] * cofactor[2][0]
    )
    return [[cofactor[across][within] / determinant for within in range(3)] for across in range(3)]


def model_terms(variance, scale):
    decay_rate = ROOT_FIVE / scale
    damping = jnp.exp(-decay_rate)
    transition = [
        [
            damping
            * (
                (1.0 if across == within else 0.0)
                + decay_rate * NILPOTENT[across][within]
                + 0.5 * decay_rate * decay_rate * NILPOTENT_SQUARED[across][within]
            )
            for within in range(3)
        ]
        for across in range(3)
    ]
    stationary = [
        [variance * STATIONARY[across][within] for within in range(3)] for across in range(3)
    ]
    carried = mat_mul(mat_mul(transition, stationary), transposed(transition))
    process_noise = [
        [stationary[across][within] - carried[across][within] for within in range(3)]
        for across in range(3)
    ]
    return (transition, stationary, process_noise)


def predict_cov(covariance, transition, process_noise):
    carried = mat_mul(mat_mul(transition, covariance), transposed(transition))
    return [
        [carried[across][within] + process_noise[across][within] for within in range(3)]
        for across in range(3)
    ]


def gain_and_cov(predicted_cov, noise):
    innovation_var = predicted_cov[0][0] + noise
    kalman_gain = [predicted_cov[across][0] / innovation_var for across in range(3)]
    covariance = [
        [
            predicted_cov[across][within] - kalman_gain[across] * predicted_cov[0][within]
            for within in range(3)
        ]
        for across in range(3)
    ]
    return (kalman_gain, covariance)


def smooth_series(spectra, noise_var, variance, scale):
    transition, stationary, process_noise = model_terms(variance, scale)
    zeros = jnp.zeros_like(variance)

    def forward(carry, inputs):
        mean_state, covariance = carry
        observed, noise = inputs
        predicted_cov = predict_cov(covariance, transition, process_noise)
        smoother_gain = mat_mul(
            mat_mul(covariance, transposed(transition)), inverted(predicted_cov)
        )
        predicted = mat_vec(transition, mean_state)
        kalman_gain, covariance = gain_and_cov(predicted_cov, noise)
        residual = observed - predicted[0]
        mean_state = [predicted[across] + kalman_gain[across] * residual for across in range(3)]
        return ((mean_state, covariance), (mean_state, smoother_gain))

    _, (means, gains) = lax.scan(forward, ([zeros, zeros, zeros], stationary), (spectra, noise_var))

    def backward(later, inputs):
        mean_state, smoother_gain = inputs
        projected = mat_vec(transition, mean_state)
        difference = [later[across] - projected[across] for across in range(3)]
        correction = mat_vec(smoother_gain, difference)
        smoothed_state = [mean_state[across] + correction[across] for across in range(3)]
        return (smoothed_state, smoothed_state[0])

    last_state = [means[across][-1] for across in range(3)]
    earlier_means = [means[across][:-1] for across in range(3)]
    next_gains = [[gains[across][within][1:] for within in range(3)] for across in range(3)]
    _, field = lax.scan(backward, last_state, (earlier_means, next_gains), reverse=True)
    return jnp.concatenate([field, last_state[0][None]], axis=0)


def per_device_general(observed, noise_var, spectral_var, time_scale):
    hours_dev, lat_dev, lon_size = observed.shape
    band_count = lax.axis_size("space")
    lat_size = lat_dev * band_count
    modes_dev = lon_size // band_count
    lon_table = lon_basis(lon_size)
    lat_table = lat_basis(lat_size).reshape(lat_size, band_count, lat_dev)
    grid_rows = observed.reshape(hours_dev * lat_dev, lon_size)
    spectra = lax.dot_general(lon_table, grid_rows, (((1,), (1,)), ((), ())), precision=HIGHEST)
    by_mode = lax.all_to_all(spectra, "space", split_axis=0, concat_axis=1, tiled=True)
    by_mode = by_mode.reshape(modes_dev, band_count, hours_dev, lat_dev)
    coefficients = jnp.einsum("msha,nsa->hmn", by_mode, lat_table, precision=HIGHEST)
    flat = coefficients.reshape(hours_dev, modes_dev * lat_size)
    hourly = lax.all_to_all(flat, "tm", split_axis=1, concat_axis=0, tiled=True)
    share = flat.shape[1] // lax.axis_size("tm")
    offset = lax.axis_index("tm") * share
    variance = lax.dynamic_slice_in_dim(spectral_var.reshape(-1), offset, share)
    scale = lax.dynamic_slice_in_dim(time_scale.reshape(-1), offset, share)
    series = smooth_series(hourly, noise_var, variance, scale)
    smooth = lax.all_to_all(series, "tm", split_axis=0, concat_axis=1, tiled=True).reshape(
        hours_dev, modes_dev, lat_size
    )
    latitude_grid = jnp.einsum("hmn,nsa->msha", smooth, lat_table, precision=HIGHEST)
    latitude_grid = latitude_grid.reshape(modes_dev, band_count * hours_dev * lat_dev)
    by_band = lax.all_to_all(latitude_grid, "space", split_axis=1, concat_axis=0, tiled=True)
    field = lax.dot_general(by_band, lon_table, (((0,), (0,)), ((), ())), precision=HIGHEST)
    return field.reshape(hours_dev, lat_dev, lon_size)


LANES = 128
ROWS = 8
MESH = pl.DeviceIdType.MESH
NT = (((1,), (1,)), ((), ()))
NN = (((1,), (0,)), ((), ()))


def round_up(value, unit):
    return -(-value // unit) * unit


def lon_tables(lon_size, times, bands, slots_used):
    half = lon_size // 2
    modes_dev = lon_size // bands
    slots = modes_dev // times
    mode = (
        np.arange(bands)[None, :, None] * modes_dev
        + np.arange(times)[:, None, None]
        + times * np.arange(slots)[None, None, :]
    )
    sine = mode > half
    frequency = np.where(sine, mode - half, mode)
    radians = (frequency[..., None] * np.arange(half) % lon_size) * (2.0 * math.pi / lon_size)
    waveform = np.where(sine[..., None], np.sin(radians), np.cos(radians))
    edge = (mode == 0) | (mode == half)
    table = waveform * np.where(edge, math.sqrt(1.0 / lon_size), math.sqrt(2.0 / lon_size))[..., None]
    full = np.zeros((times, bands, slots_used, round_up(half, LANES)), np.float32)
    full[:, :, :slots, :half] = table
    high = full.astype(jnp.bfloat16)
    low = (full - high.astype(np.float32)).astype(jnp.bfloat16)
    return high, low


def lat_tables(lat_size, bands):
    lat_dev = lat_size // bands
    wavenumber = np.arange(lat_size)[:, None]
    latitude = np.arange(lat_size)[None, :]
    radians = (wavenumber * (2 * latitude + 1) % (4 * lat_size)) * (math.pi / (2.0 * lat_size))
    table = np.cos(radians) * np.where(wavenumber == 0, math.sqrt(1.0 / lat_size), math.sqrt(2.0 / lat_size))
    full = np.zeros((lat_size, bands, ROWS), np.float32)
    full[:, :, :lat_dev] = table.reshape(lat_size, bands, lat_dev)
    full = full.reshape(lat_size, bands * ROWS)
    return full, np.ascontiguousarray(full.T)


def split(value):
    high = value.astype(jnp.bfloat16)
    low = (value - high.astype(jnp.float32)).astype(jnp.bfloat16)
    return high, low


def swap_halves(first, second):
    left = lax.broadcasted_iota(jnp.int32, first.shape, 1) < LANES // 2
    return (
        jnp.where(left, first, pltpu.roll(second, LANES // 2, 1)),
        jnp.where(left, pltpu.roll(first, LANES // 2, 1), second),
    )


def symmetric_gains(noise_ref, variance, scale, transition_ref, gain_ref, smoother_ref):
    hours = gain_ref.shape[0]
    transition, stationary, process = model_terms(variance, scale)
    pairs = [(0, 0), (0, 1), (0, 2), (1, 1), (1, 2), (2, 2)]
    for row in range(3):
        for column in range(3):
            transition_ref[row, column] = transition[row][column]

    def unpack(packed):
        matrix = [[None] * 3 for _ in range(3)]
        for (row, column), value in zip(pairs, packed):
            matrix[row][column] = matrix[column][row] = value
        return matrix

    def update(predicted, hour):
        inverse_var = 1.0 / (predicted[0][0] + noise_ref[hour])
        gain = [predicted[row][0] * inverse_var for row in range(3)]
        for row in range(3):
            gain_ref[hour, row] = gain[row]
        return [predicted[row][column] - gain[row] * predicted[0][column] for row, column in pairs]

    def step(hour, packed):
        covariance = unpack(packed)
        moved = mat_mul(transition, covariance)
        predicted = unpack(
            [
                moved[row][0] * transition[column][0]
                + moved[row][1] * transition[column][1]
                + moved[row][2] * transition[column][2]
                + process[row][column]
                for row, column in pairs
            ]
        )
        c00 = predicted[1][1] * predicted[2][2] - predicted[1][2] * predicted[1][2]
        c01 = predicted[0][2] * predicted[1][2] - predicted[0][1] * predicted[2][2]
        c02 = predicted[0][1] * predicted[1][2] - predicted[0][2] * predicted[1][1]
        c11 = predicted[0][0] * predicted[2][2] - predicted[0][2] * predicted[0][2]
        c12 = predicted[0][1] * predicted[0][2] - predicted[0][0] * predicted[1][2]
        c22 = predicted[0][0] * predicted[1][1] - predicted[0][1] * predicted[0][1]
        inverse_det = 1.0 / (predicted[0][0] * c00 + predicted[0][1] * c01 + predicted[0][2] * c02)
        cofactors = unpack([c00, c01, c02, c11, c12, c22])
        for row in range(3):
            scaled = [moved[within][row] * inverse_det for within in range(3)]
            for column in range(3):
                smoother_ref[hour - 1, row, column] = (
                    scaled[0] * cofactors[0][column]
                    + scaled[1] * cofactors[1][column]
                    + scaled[2] * cofactors[2][column]
                )
        return tuple(update(predicted, hour))

    first = tuple(update(stationary, 0))
    lax.fori_loop(1, hours, step, first)


def smoother_kernel(
    times,
    bands,
    slots_used,
    observed_hbm,
    noise_hbm,
    variance_hbm,
    scale_hbm,
    forward_lat_hbm,
    inverse_lat_hbm,
    high_hbm,
    low_hbm,
    out_ref,
    observed_ref,
    noise_ref,
    variance_ref,
    scale_ref,
    forward_lat_ref,
    inverse_lat_ref,
    high,
    low,
    folded,
    outbox,
    inbox,
    outbox_back,
    inbox_back,
    transition_ref,
    gain_ref,
    smoother_ref,
    input_sem,
    table_sem,
    send_sem,
    recv_sem,
    send_back_sem,
    recv_back_sem,
):
    devices = times * bands
    my_time = lax.axis_index("tm")
    my_band = lax.axis_index("space")
    me = my_time * bands + my_band
    lat_dev, lon_size = observed_ref.shape[0], observed_ref.shape[2]
    half = lon_size // 2
    hours = gain_ref.shape[0]
    n_half = gain_ref.shape[2]
    width = LANES // 2

    def table_copy(time, which):
        source, target = ((high_hbm, high), (low_hbm, low))[which]
        return pltpu.make_async_copy(
            source.at[time], target.at[time, :, pl.ds(0, slots_used), :], table_sem.at[time, which]
        )

    inputs = [
        pltpu.make_async_copy(source, target, input_sem.at[index])
        for index, (source, target) in enumerate(
            [
                (observed_hbm, observed_ref),
                (noise_hbm, noise_ref),
                (variance_hbm, variance_ref),
                (scale_hbm, scale_ref),
                (forward_lat_hbm, forward_lat_ref),
                (inverse_lat_hbm, inverse_lat_ref),
            ]
        )
    ]
    inputs[0].start()
    for time in range(times):
        table_copy(time, 0).start()
        table_copy(time, 1).start()
    for copy in inputs[1:]:
        copy.start()

    inbox[...] = jnp.zeros_like(inbox)
    inbox_back[...] = jnp.zeros_like(inbox_back)

    barrier = pltpu.get_barrier_semaphore()

    def greet(step, carry):
        peer = lax.rem(me + step, devices)
        pl.semaphore_signal(
            barrier, inc=1, device_id=(peer // bands, lax.rem(peer, bands)), device_id_type=MESH
        )
        return carry

    lax.fori_loop(1, devices, greet, 0)

    spare = width - slots_used
    high[:, :, slots_used:, :] = jnp.zeros((times, bands, spare, high.shape[3]), high.dtype)
    low[:, :, slots_used:, :] = jnp.zeros((times, bands, spare, low.shape[3]), low.dtype)
    folded[...] = jnp.zeros_like(folded)
    inputs[0].wait()
    for hour in range(2):
        early = observed_ref[:, hour, :half]
        late = observed_ref[:, hour, half:]
        folded[0, hour * ROWS : hour * ROWS + lat_dev, :half] = early + late
        folded[1, hour * ROWS : hour * ROWS + lat_dev, :half] = early - late
    rows = []
    for parity in range(2):
        upper, lower = split(folded[parity])
        rows.append((jnp.concatenate([upper, lower], axis=0), upper))

    def flat(ref, time):
        return ref[time].reshape(bands * width, ref.shape[3])

    for time in range(times):
        table_copy(time, 0).wait()
        table_copy(time, 1).wait()
        both, upper = rows[time % 2]
        wide = lax.dot_general(both, flat(high, time), NT, preferred_element_type=jnp.float32)
        rest = lax.dot_general(upper, flat(low, time), NT, preferred_element_type=jnp.float32)
        spectra = wide[: 2 * ROWS] + wide[2 * ROWS :] + rest
        for pair in range(bands // 2):
            block = spectra[:, pair * LANES : (pair + 1) * LANES]
            outbox[time, 2 * pair], outbox[time, 2 * pair + 1] = swap_halves(block[:ROWS], block[ROWS:])

    pl.semaphore_wait(barrier, devices - 1)

    def exchange(box, landing, sends, recvs, peer, slot):
        peer_time, peer_band = peer // bands, lax.rem(peer, bands)
        slot_time, slot_band = slot // bands, lax.rem(slot, bands)
        return pltpu.make_async_remote_copy(
            src_ref=box.at[peer_time, peer_band, pl.ds(0, lat_dev)],
            dst_ref=landing.at[slot_time, slot_band, pl.ds(0, lat_dev)],
            send_sem=sends.at[peer],
            recv_sem=recvs.at[slot],
            device_id=(peer_time, peer_band),
            device_id_type=MESH,
        )

    def send(step, carry):
        peer = lax.rem(me + step, devices)
        exchange(outbox, inbox, send_sem, recv_sem, peer, me).start()
        return carry

    def settle(step, carry):
        peer = lax.rem(me + step, devices)
        exchange(outbox, inbox, send_sem, recv_sem, peer, peer).wait()
        return carry

    lax.fori_loop(1, devices, send, 0)
    inbox[my_time, my_band] = outbox[my_time, my_band]

    for copy in inputs[1:]:
        copy.wait()
    modes_dev = variance_ref.shape[1]
    slots = modes_dev // times
    mode = lax.broadcasted_iota(jnp.int32, (modes_dev, LANES), 0)
    slot = lax.rem(lax.broadcasted_iota(jnp.int32, (modes_dev, LANES), 1), width)
    picked = ((mode == slot * times + my_time) & (slot < slots)).astype(jnp.float32)
    tile_lane = lax.broadcasted_iota(jnp.int32, (n_half, LANES), 1)

    def own_modes(ref):
        mine = lax.dot_general(ref[...], picked, NN, precision=HIGHEST, preferred_element_type=jnp.float32)
        mine = jnp.where(tile_lane < width, mine[:n_half], mine[n_half:])
        return jnp.where(lax.rem(tile_lane, width) < slots, mine, 1.0)

    symmetric_gains(
        noise_ref, own_modes(variance_ref), own_modes(scale_ref), transition_ref, gain_ref, smoother_ref
    )
    lax.fori_loop(1, devices, settle, 0)

    spectra = []
    for time in range(times):
        mixed = lax.dot_general(
            forward_lat_ref[...],
            inbox[time].reshape(bands * ROWS, LANES),
            NN,
            precision=HIGHEST,
            preferred_element_type=jnp.float32,
        )
        spectra.extend(swap_halves(mixed[:n_half], mixed[n_half:]))

    transition = [[transition_ref[row, column] for column in range(3)] for row in range(3)]
    means, predictions = [], [None]
    means.append([gain_ref[0, row] * spectra[0] for row in range(3)])
    for hour in range(1, hours):
        predicted = mat_vec(transition, means[-1])
        residual = spectra[hour] - predicted[0]
        predictions.append(predicted)
        means.append([predicted[row] + gain_ref[hour, row] * residual for row in range(3)])
    smoothed = means[-1]
    series = [None] * hours
    series[hours - 1] = smoothed[0]
    for hour in range(hours - 2, -1, -1):
        difference = [smoothed[row] - predictions[hour + 1][row] for row in range(3)]
        smoothed = [
            means[hour][row]
            + smoother_ref[hour, row, 0] * difference[0]
            + smoother_ref[hour, row, 1] * difference[1]
            + smoother_ref[hour, row, 2] * difference[2]
            for row in range(3)
        ]
        series[hour] = smoothed[0]

    for time in range(times):
        stacked = jnp.concatenate(swap_halves(series[2 * time], series[2 * time + 1]), axis=0)
        grid = lax.dot_general(
            inverse_lat_ref[...], stacked, NN, precision=HIGHEST, preferred_element_type=jnp.float32
        )
        outbox_back[time] = grid.reshape(bands, ROWS, LANES)

    def send_back(step, carry):
        peer = lax.rem(me + step, devices)
        exchange(outbox_back, inbox_back, send_back_sem, recv_back_sem, peer, me).start()
        return carry

    def settle_back(step, carry):
        peer = lax.rem(me + step, devices)
        exchange(outbox_back, inbox_back, send_back_sem, recv_back_sem, peer, peer).wait()
        return carry

    lax.fori_loop(1, devices, send_back, 0)
    inbox_back[my_time, my_band] = outbox_back[my_time, my_band]
    lax.fori_loop(1, devices, settle_back, 0)

    sums = [None, None]
    for time in range(times):
        blocks = []
        for pair in range(bands // 2):
            first, second = swap_halves(inbox_back[time, 2 * pair], inbox_back[time, 2 * pair + 1])
            blocks.append(jnp.concatenate([first, second], axis=0))
        upper, lower = split(jnp.concatenate(blocks, axis=1))
        both = jnp.concatenate([upper, lower], axis=0)
        wide = lax.dot_general(both, flat(high, time), NN, preferred_element_type=jnp.float32)
        rest = lax.dot_general(upper, flat(low, time), NN, preferred_element_type=jnp.float32)
        part = wide[: 2 * ROWS] + wide[2 * ROWS :] + rest
        sums[time % 2] = part if sums[time % 2] is None else sums[time % 2] + part
    early = sums[0] + sums[1]
    late = sums[0] - sums[1]
    for hour in range(2):
        out_ref[:, hour, :half] = early[hour * ROWS : hour * ROWS + lat_dev, :half]
        out_ref[:, hour, half:] = late[hour * ROWS : hour * ROWS + lat_dev, :half]


def per_device_fused(observed, noise_var, spectral_var, time_scale):
    times, bands = lax.axis_size("tm"), lax.axis_size("space")
    hours_dev, lat_dev, lon_size = observed.shape
    hours, lat_size = noise_var.shape[0], spectral_var.shape[1]
    slots_used = round_up(spectral_var.shape[0] // times, 2 * ROWS)
    n_half, width = lat_size // 2, LANES // 2
    half_padded = round_up(lon_size // 2, LANES)

    high, low = lon_tables(lon_size, times, bands, slots_used)
    forward_lat, inverse_lat = lat_tables(lat_size, bands)
    in_vmem = pl.BlockSpec(memory_space=pltpu.VMEM)
    in_place = pl.BlockSpec(memory_space=pltpu.HBM)
    box = pltpu.VMEM((times, bands, ROWS, LANES), jnp.float32)
    table = pltpu.VMEM((times, bands, width, half_padded), jnp.bfloat16)
    dma = pltpu.SemaphoreType.DMA
    field = pl.pallas_call(
        functools.partial(smoother_kernel, times, bands, slots_used),
        out_shape=jax.ShapeDtypeStruct((lat_dev, hours_dev, lon_size), jnp.float32),
        in_specs=[in_place] * 8,
        out_specs=in_vmem,
        scratch_shapes=[
            pltpu.VMEM((lat_dev, hours_dev, lon_size), jnp.float32),
            pltpu.SMEM((hours,), jnp.float32),
            pltpu.VMEM((lat_size, spectral_var.shape[0]), jnp.float32),
            pltpu.VMEM((lat_size, spectral_var.shape[0]), jnp.float32),
            pltpu.VMEM(forward_lat.shape, jnp.float32),
            pltpu.VMEM(inverse_lat.shape, jnp.float32),
            table,
            table,
            pltpu.VMEM((2, 2 * ROWS, half_padded), jnp.float32),
            box,
            box,
            box,
            box,
            pltpu.VMEM((3, 3, n_half, LANES), jnp.float32),
            pltpu.VMEM((hours, 3, n_half, LANES), jnp.float32),
            pltpu.VMEM((hours, 3, 3, n_half, LANES), jnp.float32),
            dma((6,)),
            dma((times, 2)),
            dma((times * bands,)),
            dma((times * bands,)),
            dma((times * bands,)),
            dma((times * bands,)),
        ],
        compiler_params=pltpu.CompilerParams(collective_id=0, has_side_effects=True),
    )(
        observed.transpose(1, 0, 2),
        noise_var,
        spectral_var.T,
        time_scale.T,
        jnp.asarray(forward_lat),
        jnp.asarray(inverse_lat),
        jnp.asarray(high),
        jnp.asarray(low),
    )
    return field.transpose(1, 0, 2)


def fits(observed, spectral_var):
    times, bands = lax.axis_size("tm"), lax.axis_size("space")
    hours_dev, lat_dev, lon_size = observed.shape
    modes_dev, lat_size = spectral_var.shape
    return (
        hours_dev == 2
        and lat_dev <= ROWS
        and lat_size % (2 * ROWS) == 0
        and bands % 2 == 0
        and times % 2 == 0
        and lon_size % 4 == 0
        and modes_dev % 2 == 0
        and modes_dev % times == 0
        and LANES // 4 < modes_dev // times <= LANES // 2
    )


def per_device(observed, noise_var, spectral_var, time_scale):
    if fits(observed, spectral_var):
        return per_device_fused(observed, noise_var, spectral_var, time_scale)
    return per_device_general(observed, noise_var, spectral_var, time_scale)


def solution(mesh):
    placed = (P("tm", "space", None), P(), P("space", None), P("space", None))
    return jax.shard_map(
        per_device, mesh=mesh, in_specs=placed, out_specs=P("tm", "space", None), check_vma=False
    )
```

```python
import functools
import math

import jax
import jax.numpy as jnp
import numpy as np
from jax import lax
from jax.experimental import pallas as pl
from jax.experimental.pallas import tpu as pltpu
from jax.sharding import PartitionSpec as P

HIGHEST = lax.Precision.HIGHEST
ROOT_FIVE = 2.23606797749979
NILPOTENT = ((1.0, 1.0, 0.0), (0.0, 1.0, 1.0), (-1.0, -3.0, -2.0))
NILPOTENT_SQUARED = ((1.0, 2.0, 1.0), (-1.0, -2.0, -1.0), (1.0, 2.0, 1.0))
STATIONARY = ((1.0, 0.0, -1.0 / 3.0), (0.0, 1.0 / 3.0, 0.0), (-1.0 / 3.0, 0.0, 1.0))


def lon_basis(size):
    mode_index = lax.broadcasted_iota(jnp.int32, (size, size), 0)
    longitude = lax.broadcasted_iota(jnp.int32, (size, size), 1)
    half_size = size // 2
    sine_rows = mode_index > half_size
    frequency = jnp.where(sine_rows, mode_index - half_size, mode_index)
    radians = (frequency * longitude % size).astype(jnp.float32) * (2.0 * math.pi / size)
    waveform = jnp.where(sine_rows, jnp.sin(radians), jnp.cos(radians))
    edge_rows = (mode_index == 0) | (mode_index == half_size)
    weight = jnp.where(edge_rows, math.sqrt(1.0 / size), math.sqrt(2.0 / size))
    return waveform * weight


def lat_basis(size):
    wavenumber = lax.broadcasted_iota(jnp.int32, (size, size), 0)
    latitude = lax.broadcasted_iota(jnp.int32, (size, size), 1)
    radians = (wavenumber * (2 * latitude + 1) % (4 * size)).astype(jnp.float32) * (
        math.pi / (2.0 * size)
    )
    weight = jnp.where(wavenumber == 0, math.sqrt(1.0 / size), math.sqrt(2.0 / size))
    return jnp.cos(radians) * weight


def mat_mul(left, right):
    return [
        [
            left[across][0] * right[0][within]
            + left[across][1] * right[1][within]
            + left[across][2] * right[2][within]
            for within in range(3)
        ]
        for across in range(3)
    ]


def mat_vec(matrix, vector):
    return [
        matrix[across][0] * vector[0]
        + matrix[across][1] * vector[1]
        + matrix[across][2] * vector[2]
        for across in range(3)
    ]


def transposed(matrix):
    return [[matrix[within][across] for within in range(3)] for across in range(3)]


def inverted(matrix):
    cofactor = [
        [
            matrix[1][1] * matrix[2][2] - matrix[1][2] * matrix[2][1],
            matrix[0][2] * matrix[2][1] - matrix[0][1] * matrix[2][2],
            matrix[0][1] * matrix[1][2] - matrix[0][2] * matrix[1][1],
        ],
        [
            matrix[1][2] * matrix[2][0] - matrix[1][0] * matrix[2][2],
            matrix[0][0] * matrix[2][2] - matrix[0][2] * matrix[2][0],
            matrix[0][2] * matrix[1][0] - matrix[0][0] * matrix[1][2],
        ],
        [
            matrix[1][0] * matrix[2][1] - matrix[1][1] * matrix[2][0],
            matrix[0][1] * matrix[2][0] - matrix[0][0] * matrix[2][1],
            matrix[0][0] * matrix[1][1] - matrix[0][1] * matrix[1][0],
        ],
    ]
    determinant = (
        matrix[0][0] * cofactor[0][0]
        + matrix[0][1] * cofactor[1][0]
        + matrix[0][2] * cofactor[2][0]
    )
    return [[cofactor[across][within] / determinant for within in range(3)] for across in range(3)]


def model_terms(variance, scale):
    decay_rate = ROOT_FIVE / scale
    damping = jnp.exp(-decay_rate)
    transition = [
        [
            damping
            * (
                (1.0 if across == within else 0.0)
                + decay_rate * NILPOTENT[across][within]
                + 0.5 * decay_rate * decay_rate * NILPOTENT_SQUARED[across][within]
            )
            for within in range(3)
        ]
        for across in range(3)
    ]
    stationary = [
        [variance * STATIONARY[across][within] for within in range(3)] for across in range(3)
    ]
    carried = mat_mul(mat_mul(transition, stationary), transposed(transition))
    process_noise = [
        [stationary[across][within] - carried[across][within] for within in range(3)]
        for across in range(3)
    ]
    return (transition, stationary, process_noise)


def predict_cov(covariance, transition, process_noise):
    carried = mat_mul(mat_mul(transition, covariance), transposed(transition))
    return [
        [carried[across][within] + process_noise[across][within] for within in range(3)]
        for across in range(3)
    ]


def gain_and_cov(predicted_cov, noise):
    innovation_var = predicted_cov[0][0] + noise
    kalman_gain = [predicted_cov[across][0] / innovation_var for across in range(3)]
    covariance = [
        [
            predicted_cov[across][within] - kalman_gain[across] * predicted_cov[0][within]
            for within in range(3)
        ]
        for across in range(3)
    ]
    return (kalman_gain, covariance)


def smooth_series(spectra, noise_var, variance, scale):
    transition, stationary, process_noise = model_terms(variance, scale)
    zeros = jnp.zeros_like(variance)

    def forward(carry, inputs):
        mean_state, covariance = carry
        observed, noise = inputs
        predicted_cov = predict_cov(covariance, transition, process_noise)
        smoother_gain = mat_mul(
            mat_mul(covariance, transposed(transition)), inverted(predicted_cov)
        )
        predicted = mat_vec(transition, mean_state)
        kalman_gain, covariance = gain_and_cov(predicted_cov, noise)
        residual = observed - predicted[0]
        mean_state = [predicted[across] + kalman_gain[across] * residual for across in range(3)]
        return ((mean_state, covariance), (mean_state, smoother_gain))

    _, (means, gains) = lax.scan(forward, ([zeros, zeros, zeros], stationary), (spectra, noise_var))

    def backward(later, inputs):
        mean_state, smoother_gain = inputs
        projected = mat_vec(transition, mean_state)
        difference = [later[across] - projected[across] for across in range(3)]
        correction = mat_vec(smoother_gain, difference)
        smoothed_state = [mean_state[across] + correction[across] for across in range(3)]
        return (smoothed_state, smoothed_state[0])

    last_state = [means[across][-1] for across in range(3)]
    earlier_means = [means[across][:-1] for across in range(3)]
    next_gains = [[gains[across][within][1:] for within in range(3)] for across in range(3)]
    _, field = lax.scan(backward, last_state, (earlier_means, next_gains), reverse=True)
    return jnp.concatenate([field, last_state[0][None]], axis=0)


def per_device_general(observed, noise_var, spectral_var, time_scale):
    hours_dev, lat_dev, lon_size = observed.shape
    band_count = lax.axis_size("space")
    lat_size = lat_dev * band_count
    modes_dev = lon_size // band_count
    lon_table = lon_basis(lon_size)
    lat_table = lat_basis(lat_size).reshape(lat_size, band_count, lat_dev)
    grid_rows = observed.reshape(hours_dev * lat_dev, lon_size)
    spectra = lax.dot_general(lon_table, grid_rows, (((1,), (1,)), ((), ())), precision=HIGHEST)
    by_mode = lax.all_to_all(spectra, "space", split_axis=0, concat_axis=1, tiled=True)
    by_mode = by_mode.reshape(modes_dev, band_count, hours_dev, lat_dev)
    coefficients = jnp.einsum("msha,nsa->hmn", by_mode, lat_table, precision=HIGHEST)
    flat = coefficients.reshape(hours_dev, modes_dev * lat_size)
    hourly = lax.all_to_all(flat, "tm", split_axis=1, concat_axis=0, tiled=True)
    share = flat.shape[1] // lax.axis_size("tm")
    offset = lax.axis_index("tm") * share
    variance = lax.dynamic_slice_in_dim(spectral_var.reshape(-1), offset, share)
    scale = lax.dynamic_slice_in_dim(time_scale.reshape(-1), offset, share)
    series = smooth_series(hourly, noise_var, variance, scale)
    smooth = lax.all_to_all(series, "tm", split_axis=0, concat_axis=1, tiled=True).reshape(
        hours_dev, modes_dev, lat_size
    )
    latitude_grid = jnp.einsum("hmn,nsa->msha", smooth, lat_table, precision=HIGHEST)
    latitude_grid = latitude_grid.reshape(modes_dev, band_count * hours_dev * lat_dev)
    by_band = lax.all_to_all(latitude_grid, "space", split_axis=1, concat_axis=0, tiled=True)
    field = lax.dot_general(by_band, lon_table, (((0,), (0,)), ((), ())), precision=HIGHEST)
    return field.reshape(hours_dev, lat_dev, lon_size)


LANES = 128
ROWS = 8
MESH = pl.DeviceIdType.MESH
NT = (((1,), (1,)), ((), ()))
NN = (((1,), (0,)), ((), ()))


def round_up(value, unit):
    return -(-value // unit) * unit


def lon_tables(lon_size, times, bands, slots_used):
    half = lon_size // 2
    modes_dev = lon_size // bands
    slots = modes_dev // times
    mode = (
        np.arange(bands)[None, :, None] * modes_dev
        + np.arange(times)[:, None, None]
        + times * np.arange(slots)[None, None, :]
    )
    sine = mode > half
    frequency = np.where(sine, mode - half, mode)
    radians = (frequency[..., None] * np.arange(half) % lon_size) * (2.0 * math.pi / lon_size)
    waveform = np.where(sine[..., None], np.sin(radians), np.cos(radians))
    edge = (mode == 0) | (mode == half)
    table = waveform * np.where(edge, math.sqrt(1.0 / lon_size), math.sqrt(2.0 / lon_size))[..., None]
    full = np.zeros((times, bands, slots_used, round_up(half, LANES)), np.float32)
    full[:, :, :slots, :half] = table
    high = full.astype(jnp.bfloat16)
    low = (full - high.astype(np.float32)).astype(jnp.bfloat16)
    return high, low


def lat_tables(lat_size, bands):
    lat_dev = lat_size // bands
    wavenumber = np.arange(lat_size)[:, None]
    latitude = np.arange(lat_size)[None, :]
    radians = (wavenumber * (2 * latitude + 1) % (4 * lat_size)) * (math.pi / (2.0 * lat_size))
    table = np.cos(radians) * np.where(wavenumber == 0, math.sqrt(1.0 / lat_size), math.sqrt(2.0 / lat_size))
    full = np.zeros((lat_size, bands, ROWS), np.float32)
    full[:, :, :lat_dev] = table.reshape(lat_size, bands, lat_dev)
    full = full.reshape(lat_size, bands * ROWS)

    def stacked(array):
        high = array.astype(jnp.bfloat16)
        return np.concatenate([high, (array - high.astype(np.float32)).astype(jnp.bfloat16)], axis=0)

    return stacked(full), stacked(np.ascontiguousarray(full.T))


def split(value):
    high = value.astype(jnp.bfloat16)
    low = (value - high.astype(jnp.float32)).astype(jnp.bfloat16)
    return high, low


def paired_dot(table, value):
    both = jnp.concatenate(split(value), axis=1)
    product = lax.dot_general(table, both, NN, preferred_element_type=jnp.float32)
    rows = table.shape[0] // 2
    return product[:rows, :LANES] + (product[:rows, LANES:] + product[rows:, :LANES])


def swap_halves(first, second):
    left = lax.broadcasted_iota(jnp.int32, first.shape, 1) < LANES // 2
    return (
        jnp.where(left, first, pltpu.roll(second, LANES // 2, 1)),
        jnp.where(left, pltpu.roll(first, LANES // 2, 1), second),
    )


def symmetric_gains(noise_ref, variance, scale, transition_ref, gain_ref, smoother_ref):
    hours = gain_ref.shape[0]
    transition, stationary, process = model_terms(variance, scale)
    pairs = [(0, 0), (0, 1), (0, 2), (1, 1), (1, 2), (2, 2)]
    for row in range(3):
        for column in range(3):
            transition_ref[row, column] = transition[row][column]

    def unpack(packed):
        matrix = [[None] * 3 for _ in range(3)]
        for (row, column), value in zip(pairs, packed):
            matrix[row][column] = matrix[column][row] = value
        return matrix

    def update(predicted, hour):
        inverse_var = 1.0 / (predicted[0][0] + noise_ref[hour])
        gain = [predicted[row][0] * inverse_var for row in range(3)]
        for row in range(3):
            gain_ref[hour, row] = gain[row]
        return [predicted[row][column] - gain[row] * predicted[0][column] for row, column in pairs]

    def step(hour, packed):
        covariance = unpack(packed)
        moved = mat_mul(transition, covariance)
        predicted = unpack(
            [
                moved[row][0] * transition[column][0]
                + moved[row][1] * transition[column][1]
                + moved[row][2] * transition[column][2]
                + process[row][column]
                for row, column in pairs
            ]
        )
        c00 = predicted[1][1] * predicted[2][2] - predicted[1][2] * predicted[1][2]
        c01 = predicted[0][2] * predicted[1][2] - predicted[0][1] * predicted[2][2]
        c02 = predicted[0][1] * predicted[1][2] - predicted[0][2] * predicted[1][1]
        c11 = predicted[0][0] * predicted[2][2] - predicted[0][2] * predicted[0][2]
        c12 = predicted[0][1] * predicted[0][2] - predicted[0][0] * predicted[1][2]
        c22 = predicted[0][0] * predicted[1][1] - predicted[0][1] * predicted[0][1]
        inverse_det = 1.0 / (predicted[0][0] * c00 + predicted[0][1] * c01 + predicted[0][2] * c02)
        cofactors = unpack([c00, c01, c02, c11, c12, c22])
        for row in range(3):
            scaled = [moved[within][row] * inverse_det for within in range(3)]
            for column in range(3):
                smoother_ref[hour - 1, row, column] = (
                    scaled[0] * cofactors[0][column]
                    + scaled[1] * cofactors[1][column]
                    + scaled[2] * cofactors[2][column]
                )
        return tuple(update(predicted, hour))

    first = tuple(update(stationary, 0))
    lax.fori_loop(1, hours, step, first)


def smoother_kernel(
    times,
    bands,
    slots_used,
    observed_hbm,
    noise_hbm,
    variance_hbm,
    scale_hbm,
    forward_lat_hbm,
    inverse_lat_hbm,
    high_hbm,
    low_hbm,
    out_ref,
    observed_ref,
    noise_ref,
    variance_ref,
    scale_ref,
    forward_lat_ref,
    inverse_lat_ref,
    high,
    low,
    folded,
    outbox,
    inbox,
    outbox_back,
    inbox_back,
    transition_ref,
    gain_ref,
    smoother_ref,
    input_sem,
    table_sem,
    send_sem,
    recv_sem,
    send_back_sem,
    recv_back_sem,
):
    devices = times * bands
    my_time = lax.axis_index("tm")
    my_band = lax.axis_index("space")
    me = my_time * bands + my_band
    lat_dev, lon_size = observed_ref.shape[0], observed_ref.shape[2]
    half = lon_size // 2
    hours = gain_ref.shape[0]
    n_half = gain_ref.shape[2]
    width = LANES // 2

    def table_copy(time, which):
        source, target = ((high_hbm, high), (low_hbm, low))[which]
        return pltpu.make_async_copy(
            source.at[time], target.at[time, :, pl.ds(0, slots_used), :], table_sem.at[time, which]
        )

    inputs = [
        pltpu.make_async_copy(source, target, input_sem.at[index])
        for index, (source, target) in enumerate(
            [
                (observed_hbm, observed_ref),
                (noise_hbm, noise_ref),
                (variance_hbm, variance_ref),
                (scale_hbm, scale_ref),
                (forward_lat_hbm, forward_lat_ref),
                (inverse_lat_hbm, inverse_lat_ref),
            ]
        )
    ]
    inputs[0].start()
    for time in range(times):
        table_copy(time, 0).start()
        table_copy(time, 1).start()
    for copy in inputs[1:]:
        copy.start()

    inbox[...] = jnp.zeros_like(inbox)
    inbox_back[...] = jnp.zeros_like(inbox_back)

    barrier = pltpu.get_barrier_semaphore()

    def greet(step, carry):
        peer = lax.rem(me + step, devices)
        pl.semaphore_signal(
            barrier, inc=1, device_id=(peer // bands, lax.rem(peer, bands)), device_id_type=MESH
        )
        return carry

    lax.fori_loop(1, devices, greet, 0)

    spare = width - slots_used
    high[:, :, slots_used:, :] = jnp.zeros((times, bands, spare, high.shape[3]), high.dtype)
    low[:, :, slots_used:, :] = jnp.zeros((times, bands, spare, low.shape[3]), low.dtype)
    folded[...] = jnp.zeros_like(folded)
    inputs[0].wait()
    for hour in range(2):
        early = observed_ref[:, hour, :half]
        late = observed_ref[:, hour, half:]
        folded[0, hour * ROWS : hour * ROWS + lat_dev, :half] = early + late
        folded[1, hour * ROWS : hour * ROWS + lat_dev, :half] = early - late
    rows = []
    for parity in range(2):
        upper, lower = split(folded[parity])
        rows.append((jnp.concatenate([upper, lower], axis=0), upper))

    def flat(ref, time):
        return ref[time].reshape(bands * width, ref.shape[3])

    for time in range(times):
        table_copy(time, 0).wait()
        table_copy(time, 1).wait()
        both, upper = rows[time % 2]
        wide = lax.dot_general(both, flat(high, time), NT, preferred_element_type=jnp.float32)
        rest = lax.dot_general(upper, flat(low, time), NT, preferred_element_type=jnp.float32)
        spectra = wide[: 2 * ROWS] + wide[2 * ROWS :] + rest
        for pair in range(bands // 2):
            block = spectra[:, pair * LANES : (pair + 1) * LANES]
            owner = time * bands + 2 * pair
            outbox[owner], outbox[owner + 1] = swap_halves(block[:ROWS], block[ROWS:])

    pl.semaphore_wait(barrier, devices - 1)

    def exchange(box, landing, sends, recvs, peer, slot):
        return pltpu.make_async_remote_copy(
            src_ref=box.at[peer, pl.ds(0, lat_dev)],
            dst_ref=landing.at[slot, pl.ds(0, lat_dev)],
            send_sem=sends.at[0],
            recv_sem=recvs.at[slot // bands],
            device_id=(peer // bands, lax.rem(peer, bands)),
            device_id_type=MESH,
        )

    def send(step, carry):
        peer = lax.rem(me + step, devices)
        exchange(outbox, inbox, send_sem, recv_sem, peer, me).start()
        return carry

    def sent(box, sends):
        gone = box.at[pl.ds(0, devices - 1), pl.ds(0, lat_dev)]
        pltpu.make_async_copy(gone, gone, sends.at[0]).wait()

    def arrive(landing, recvs, step):
        time = lax.rem(my_time + step, times)
        come = landing.at[pl.ds(0, bands - 1 if step == 0 else bands), pl.ds(0, lat_dev)]
        pltpu.make_async_copy(come, come, recvs.at[time]).wait()
        return time

    lax.fori_loop(1, devices, send, 0)
    inbox[me] = outbox[me]

    for copy in inputs[1:]:
        copy.wait()
    modes_dev = variance_ref.shape[1]
    slots = modes_dev // times
    mode = lax.broadcasted_iota(jnp.int32, (modes_dev, LANES), 0)
    slot = lax.rem(lax.broadcasted_iota(jnp.int32, (modes_dev, LANES), 1), width)
    picked = ((mode == slot * times + my_time) & (slot < slots)).astype(jnp.float32)
    tile_lane = lax.broadcasted_iota(jnp.int32, (n_half, LANES), 1)

    def own_modes(ref):
        mine = lax.dot_general(ref[...], picked, NN, precision=HIGHEST, preferred_element_type=jnp.float32)
        mine = jnp.where(tile_lane < width, mine[:n_half], mine[n_half:])
        return jnp.where(lax.rem(tile_lane, width) < slots, mine, 1.0)

    symmetric_gains(
        noise_ref, own_modes(variance_ref), own_modes(scale_ref), transition_ref, gain_ref, smoother_ref
    )
    sent(outbox, send_sem)
    for step in range(times):
        arrive(inbox, recv_sem, step)

    spectra = []
    for time in range(times):
        arrived = inbox[time * bands : (time + 1) * bands].reshape(bands * ROWS, LANES)
        mixed = paired_dot(forward_lat_ref[...], arrived)
        spectra.extend(swap_halves(mixed[:n_half], mixed[n_half:]))

    transition = [[transition_ref[row, column] for column in range(3)] for row in range(3)]
    means, predictions = [], [None]
    means.append([gain_ref[0, row] * spectra[0] for row in range(3)])
    for hour in range(1, hours):
        predicted = mat_vec(transition, means[-1])
        residual = spectra[hour] - predicted[0]
        predictions.append(predicted)
        means.append([predicted[row] + gain_ref[hour, row] * residual for row in range(3)])
    smoothed = means[-1]
    series = [None] * hours
    series[hours - 1] = smoothed[0]
    for hour in range(hours - 2, -1, -1):
        difference = [smoothed[row] - predictions[hour + 1][row] for row in range(3)]
        smoothed = [
            means[hour][row]
            + smoother_ref[hour, row, 0] * difference[0]
            + smoother_ref[hour, row, 1] * difference[1]
            + smoother_ref[hour, row, 2] * difference[2]
            for row in range(3)
        ]
        series[hour] = smoothed[0]

    for time in range(times):
        stacked = jnp.concatenate(swap_halves(series[2 * time], series[2 * time + 1]), axis=0)
        grid = paired_dot(inverse_lat_ref[...], stacked)
        outbox_back[time * bands : (time + 1) * bands] = grid.reshape(bands, ROWS, LANES)

    def send_back(step, carry):
        peer = lax.rem(me + step, devices)
        exchange(outbox_back, inbox_back, send_back_sem, recv_back_sem, peer, me).start()
        return carry

    lax.fori_loop(1, devices, send_back, 0)
    inbox_back[me] = outbox_back[me]

    early = late = 0.0
    for step in range(times):
        time = arrive(inbox_back, recv_back_sem, step)
        blocks = []
        for pair in range(bands // 2):
            owner = time * bands + 2 * pair
            first, second = swap_halves(inbox_back[owner], inbox_back[owner + 1])
            blocks.append(jnp.concatenate([first, second], axis=0))
        upper, lower = split(jnp.concatenate(blocks, axis=1))
        both = jnp.concatenate([upper, lower], axis=0)
        wide = lax.dot_general(both, flat(high, time), NN, preferred_element_type=jnp.float32)
        rest = lax.dot_general(upper, flat(low, time), NN, preferred_element_type=jnp.float32)
        part = wide[: 2 * ROWS] + wide[2 * ROWS :] + rest
        early = early + part
        late = late + jnp.where(lax.rem(time, 2) == 0, part, -part)
    sent(outbox_back, send_back_sem)
    for hour in range(2):
        out_ref[:, hour, :half] = early[hour * ROWS : hour * ROWS + lat_dev, :half]
        out_ref[:, hour, half:] = late[hour * ROWS : hour * ROWS + lat_dev, :half]


def per_device_fused(observed, noise_var, spectral_var, time_scale):
    times, bands = lax.axis_size("tm"), lax.axis_size("space")
    hours_dev, lat_dev, lon_size = observed.shape
    hours, lat_size = noise_var.shape[0], spectral_var.shape[1]
    slots_used = round_up(spectral_var.shape[0] // times, 2 * ROWS)
    n_half, width = lat_size // 2, LANES // 2
    half_padded = round_up(lon_size // 2, LANES)

    high, low = lon_tables(lon_size, times, bands, slots_used)
    forward_lat, inverse_lat = lat_tables(lat_size, bands)
    in_vmem = pl.BlockSpec(memory_space=pltpu.VMEM)
    in_place = pl.BlockSpec(memory_space=pltpu.HBM)
    box = pltpu.VMEM((times * bands, ROWS, LANES), jnp.float32)
    table = pltpu.VMEM((times, bands, width, half_padded), jnp.bfloat16)
    dma = pltpu.SemaphoreType.DMA
    field = pl.pallas_call(
        functools.partial(smoother_kernel, times, bands, slots_used),
        out_shape=pltpu.VMEM((lat_dev, hours_dev, lon_size), jnp.float32),
        in_specs=[in_place] * 8,
        out_specs=in_vmem,
        scratch_shapes=[
            pltpu.VMEM((lat_dev, hours_dev, lon_size), jnp.float32),
            pltpu.SMEM((hours,), jnp.float32),
            pltpu.VMEM((lat_size, spectral_var.shape[0]), jnp.float32),
            pltpu.VMEM((lat_size, spectral_var.shape[0]), jnp.float32),
            pltpu.VMEM(forward_lat.shape, jnp.bfloat16),
            pltpu.VMEM(inverse_lat.shape, jnp.bfloat16),
            table,
            table,
            pltpu.VMEM((2, 2 * ROWS, half_padded), jnp.float32),
            box,
            box,
            box,
            box,
            pltpu.VMEM((3, 3, n_half, LANES), jnp.float32),
            pltpu.VMEM((hours, 3, n_half, LANES), jnp.float32),
            pltpu.VMEM((hours, 3, 3, n_half, LANES), jnp.float32),
            dma((6,)),
            dma((times, 2)),
            dma((1,)),
            dma((times,)),
            dma((1,)),
            dma((times,)),
        ],
        compiler_params=pltpu.CompilerParams(collective_id=0, has_side_effects=True),
    )(
        observed.transpose(1, 0, 2),
        noise_var,
        spectral_var.T,
        time_scale.T,
        jnp.asarray(forward_lat),
        jnp.asarray(inverse_lat),
        jnp.asarray(high),
        jnp.asarray(low),
    )
    return field.transpose(1, 0, 2)


def fits(observed, spectral_var):
    times, bands = lax.axis_size("tm"), lax.axis_size("space")
    hours_dev, lat_dev, lon_size = observed.shape
    modes_dev, lat_size = spectral_var.shape
    return (
        hours_dev == 2
        and lat_dev <= ROWS
        and lat_size % (2 * ROWS) == 0
        and bands % 2 == 0
        and times % 2 == 0
        and lon_size % 4 == 0
        and modes_dev % 2 == 0
        and modes_dev % times == 0
        and LANES // 4 < modes_dev // times <= LANES // 2
    )


def per_device(observed, noise_var, spectral_var, time_scale):
    if fits(observed, spectral_var):
        return per_device_fused(observed, noise_var, spectral_var, time_scale)
    return per_device_general(observed, noise_var, spectral_var, time_scale)


def solution(mesh):
    placed = (P("tm", "space", None), P(), P("space", None), P("space", None))
    return jax.shard_map(
        per_device, mesh=mesh, in_specs=placed, out_specs=P("tm", "space", None), check_vma=False
    )
```

```python
import functools
import math

import jax
import jax.numpy as jnp
import numpy as np
from jax import lax
from jax.experimental import pallas as pl
from jax.experimental.pallas import tpu as pltpu
from jax.sharding import PartitionSpec as P

HIGHEST = lax.Precision.HIGHEST
ROOT_FIVE = 2.23606797749979
NILPOTENT = ((1.0, 1.0, 0.0), (0.0, 1.0, 1.0), (-1.0, -3.0, -2.0))
NILPOTENT_SQUARED = ((1.0, 2.0, 1.0), (-1.0, -2.0, -1.0), (1.0, 2.0, 1.0))
STATIONARY = ((1.0, 0.0, -1.0 / 3.0), (0.0, 1.0 / 3.0, 0.0), (-1.0 / 3.0, 0.0, 1.0))


def lon_basis(size):
    mode_index = lax.broadcasted_iota(jnp.int32, (size, size), 0)
    longitude = lax.broadcasted_iota(jnp.int32, (size, size), 1)
    half_size = size // 2
    sine_rows = mode_index > half_size
    frequency = jnp.where(sine_rows, mode_index - half_size, mode_index)
    radians = (frequency * longitude % size).astype(jnp.float32) * (2.0 * math.pi / size)
    waveform = jnp.where(sine_rows, jnp.sin(radians), jnp.cos(radians))
    edge_rows = (mode_index == 0) | (mode_index == half_size)
    weight = jnp.where(edge_rows, math.sqrt(1.0 / size), math.sqrt(2.0 / size))
    return waveform * weight


def lat_basis(size):
    wavenumber = lax.broadcasted_iota(jnp.int32, (size, size), 0)
    latitude = lax.broadcasted_iota(jnp.int32, (size, size), 1)
    radians = (wavenumber * (2 * latitude + 1) % (4 * size)).astype(jnp.float32) * (
        math.pi / (2.0 * size)
    )
    weight = jnp.where(wavenumber == 0, math.sqrt(1.0 / size), math.sqrt(2.0 / size))
    return jnp.cos(radians) * weight


def mat_mul(left, right):
    return [
        [
            left[across][0] * right[0][within]
            + left[across][1] * right[1][within]
            + left[across][2] * right[2][within]
            for within in range(3)
        ]
        for across in range(3)
    ]


def mat_vec(matrix, vector):
    return [
        matrix[across][0] * vector[0]
        + matrix[across][1] * vector[1]
        + matrix[across][2] * vector[2]
        for across in range(3)
    ]


def transposed(matrix):
    return [[matrix[within][across] for within in range(3)] for across in range(3)]


def inverted(matrix):
    cofactor = [
        [
            matrix[1][1] * matrix[2][2] - matrix[1][2] * matrix[2][1],
            matrix[0][2] * matrix[2][1] - matrix[0][1] * matrix[2][2],
            matrix[0][1] * matrix[1][2] - matrix[0][2] * matrix[1][1],
        ],
        [
            matrix[1][2] * matrix[2][0] - matrix[1][0] * matrix[2][2],
            matrix[0][0] * matrix[2][2] - matrix[0][2] * matrix[2][0],
            matrix[0][2] * matrix[1][0] - matrix[0][0] * matrix[1][2],
        ],
        [
            matrix[1][0] * matrix[2][1] - matrix[1][1] * matrix[2][0],
            matrix[0][1] * matrix[2][0] - matrix[0][0] * matrix[2][1],
            matrix[0][0] * matrix[1][1] - matrix[0][1] * matrix[1][0],
        ],
    ]
    determinant = (
        matrix[0][0] * cofactor[0][0]
        + matrix[0][1] * cofactor[1][0]
        + matrix[0][2] * cofactor[2][0]
    )
    return [[cofactor[across][within] / determinant for within in range(3)] for across in range(3)]


def model_terms(variance, scale):
    decay_rate = ROOT_FIVE / scale
    damping = jnp.exp(-decay_rate)
    transition = [
        [
            damping
            * (
                (1.0 if across == within else 0.0)
                + decay_rate * NILPOTENT[across][within]
                + 0.5 * decay_rate * decay_rate * NILPOTENT_SQUARED[across][within]
            )
            for within in range(3)
        ]
        for across in range(3)
    ]
    stationary = [
        [variance * STATIONARY[across][within] for within in range(3)] for across in range(3)
    ]
    carried = mat_mul(mat_mul(transition, stationary), transposed(transition))
    process_noise = [
        [stationary[across][within] - carried[across][within] for within in range(3)]
        for across in range(3)
    ]
    return (transition, stationary, process_noise)


def predict_cov(covariance, transition, process_noise):
    carried = mat_mul(mat_mul(transition, covariance), transposed(transition))
    return [
        [carried[across][within] + process_noise[across][within] for within in range(3)]
        for across in range(3)
    ]


def gain_and_cov(predicted_cov, noise):
    innovation_var = predicted_cov[0][0] + noise
    kalman_gain = [predicted_cov[across][0] / innovation_var for across in range(3)]
    covariance = [
        [
            predicted_cov[across][within] - kalman_gain[across] * predicted_cov[0][within]
            for within in range(3)
        ]
        for across in range(3)
    ]
    return (kalman_gain, covariance)


def smooth_series(spectra, noise_var, variance, scale):
    transition, stationary, process_noise = model_terms(variance, scale)
    zeros = jnp.zeros_like(variance)

    def forward(carry, inputs):
        mean_state, covariance = carry
        observed, noise = inputs
        predicted_cov = predict_cov(covariance, transition, process_noise)
        smoother_gain = mat_mul(
            mat_mul(covariance, transposed(transition)), inverted(predicted_cov)
        )
        predicted = mat_vec(transition, mean_state)
        kalman_gain, covariance = gain_and_cov(predicted_cov, noise)
        residual = observed - predicted[0]
        mean_state = [predicted[across] + kalman_gain[across] * residual for across in range(3)]
        return ((mean_state, covariance), (mean_state, smoother_gain))

    _, (means, gains) = lax.scan(forward, ([zeros, zeros, zeros], stationary), (spectra, noise_var))

    def backward(later, inputs):
        mean_state, smoother_gain = inputs
        projected = mat_vec(transition, mean_state)
        difference = [later[across] - projected[across] for across in range(3)]
        correction = mat_vec(smoother_gain, difference)
        smoothed_state = [mean_state[across] + correction[across] for across in range(3)]
        return (smoothed_state, smoothed_state[0])

    last_state = [means[across][-1] for across in range(3)]
    earlier_means = [means[across][:-1] for across in range(3)]
    next_gains = [[gains[across][within][1:] for within in range(3)] for across in range(3)]
    _, field = lax.scan(backward, last_state, (earlier_means, next_gains), reverse=True)
    return jnp.concatenate([field, last_state[0][None]], axis=0)


def per_device_general(observed, noise_var, spectral_var, time_scale):
    hours_dev, lat_dev, lon_size = observed.shape
    band_count = lax.axis_size("space")
    lat_size = lat_dev * band_count
    modes_dev = lon_size // band_count
    lon_table = lon_basis(lon_size)
    lat_table = lat_basis(lat_size).reshape(lat_size, band_count, lat_dev)
    grid_rows = observed.reshape(hours_dev * lat_dev, lon_size)
    spectra = lax.dot_general(lon_table, grid_rows, (((1,), (1,)), ((), ())), precision=HIGHEST)
    by_mode = lax.all_to_all(spectra, "space", split_axis=0, concat_axis=1, tiled=True)
    by_mode = by_mode.reshape(modes_dev, band_count, hours_dev, lat_dev)
    coefficients = jnp.einsum("msha,nsa->hmn", by_mode, lat_table, precision=HIGHEST)
    flat = coefficients.reshape(hours_dev, modes_dev * lat_size)
    hourly = lax.all_to_all(flat, "tm", split_axis=1, concat_axis=0, tiled=True)
    share = flat.shape[1] // lax.axis_size("tm")
    offset = lax.axis_index("tm") * share
    variance = lax.dynamic_slice_in_dim(spectral_var.reshape(-1), offset, share)
    scale = lax.dynamic_slice_in_dim(time_scale.reshape(-1), offset, share)
    series = smooth_series(hourly, noise_var, variance, scale)
    smooth = lax.all_to_all(series, "tm", split_axis=0, concat_axis=1, tiled=True).reshape(
        hours_dev, modes_dev, lat_size
    )
    latitude_grid = jnp.einsum("hmn,nsa->msha", smooth, lat_table, precision=HIGHEST)
    latitude_grid = latitude_grid.reshape(modes_dev, band_count * hours_dev * lat_dev)
    by_band = lax.all_to_all(latitude_grid, "space", split_axis=1, concat_axis=0, tiled=True)
    field = lax.dot_general(by_band, lon_table, (((0,), (0,)), ((), ())), precision=HIGHEST)
    return field.reshape(hours_dev, lat_dev, lon_size)


LANES = 128
ROWS = 8
MESH = pl.DeviceIdType.MESH
NT = (((1,), (1,)), ((), ()))
NN = (((1,), (0,)), ((), ()))


def round_up(value, unit):
    return -(-value // unit) * unit


def lon_tables(lon_size, times, bands, slots_used):
    half = lon_size // 2
    modes_dev = lon_size // bands
    slots = modes_dev // times
    mode = (
        np.arange(bands)[None, :, None] * modes_dev
        + np.arange(times)[:, None, None]
        + times * np.arange(slots)[None, None, :]
    )
    sine = mode > half
    frequency = np.where(sine, mode - half, mode)
    radians = (frequency[..., None] * np.arange(half) % lon_size) * (2.0 * math.pi / lon_size)
    waveform = np.where(sine[..., None], np.sin(radians), np.cos(radians))
    edge = (mode == 0) | (mode == half)
    table = waveform * np.where(edge, math.sqrt(1.0 / lon_size), math.sqrt(2.0 / lon_size))[..., None]
    full = np.zeros((times, bands, slots_used, round_up(half, LANES)), np.float32)
    full[:, :, :slots, :half] = table
    high = full.astype(jnp.bfloat16)
    low = (full - high.astype(np.float32)).astype(jnp.bfloat16)
    return high, low


def lat_tables(lat_size, bands):
    lat_dev = lat_size // bands
    wavenumber = np.arange(lat_size)[:, None]
    latitude = np.arange(lat_size)[None, :]
    radians = (wavenumber * (2 * latitude + 1) % (4 * lat_size)) * (math.pi / (2.0 * lat_size))
    table = np.cos(radians) * np.where(wavenumber == 0, math.sqrt(1.0 / lat_size), math.sqrt(2.0 / lat_size))
    full = np.zeros((lat_size, bands, ROWS), np.float32)
    full[:, :, :lat_dev] = table.reshape(lat_size, bands, lat_dev)
    full = full.reshape(lat_size, bands * ROWS)

    def stacked(array):
        high = array.astype(jnp.bfloat16)
        return np.concatenate([high, (array - high.astype(np.float32)).astype(jnp.bfloat16)], axis=0)

    return stacked(full), stacked(np.ascontiguousarray(full.T))


def split(value):
    high = value.astype(jnp.bfloat16)
    low = (value - high.astype(jnp.float32)).astype(jnp.bfloat16)
    return high, low


def paired_dot(table, value):
    both = jnp.concatenate(split(value), axis=1)
    product = lax.dot_general(table, both, NN, preferred_element_type=jnp.float32)
    rows = table.shape[0] // 2
    return product[:rows, :LANES] + (product[:rows, LANES:] + product[rows:, :LANES])


def swap_halves(first, second):
    left = lax.broadcasted_iota(jnp.int32, first.shape, 1) < LANES // 2
    return (
        jnp.where(left, first, pltpu.roll(second, LANES // 2, 1)),
        jnp.where(left, pltpu.roll(first, LANES // 2, 1), second),
    )


def symmetric_gains(noise_ref, variance, scale, transition_ref, gain_ref, smoother_ref):
    hours = gain_ref.shape[0]
    transition, stationary, process = model_terms(variance, scale)
    pairs = [(0, 0), (0, 1), (0, 2), (1, 1), (1, 2), (2, 2)]
    for row in range(3):
        for column in range(3):
            transition_ref[row, column] = transition[row][column]

    def unpack(packed):
        matrix = [[None] * 3 for _ in range(3)]
        for (row, column), value in zip(pairs, packed):
            matrix[row][column] = matrix[column][row] = value
        return matrix

    def update(predicted, hour):
        inverse_var = 1.0 / (predicted[0][0] + noise_ref[hour])
        gain = [predicted[row][0] * inverse_var for row in range(3)]
        for row in range(3):
            gain_ref[hour, row] = gain[row]
        return [predicted[row][column] - gain[row] * predicted[0][column] for row, column in pairs]

    def step(hour, packed):
        covariance = unpack(packed)
        moved = mat_mul(transition, covariance)
        predicted = unpack(
            [
                moved[row][0] * transition[column][0]
                + moved[row][1] * transition[column][1]
                + moved[row][2] * transition[column][2]
                + process[row][column]
                for row, column in pairs
            ]
        )
        c00 = predicted[1][1] * predicted[2][2] - predicted[1][2] * predicted[1][2]
        c01 = predicted[0][2] * predicted[1][2] - predicted[0][1] * predicted[2][2]
        c02 = predicted[0][1] * predicted[1][2] - predicted[0][2] * predicted[1][1]
        c11 = predicted[0][0] * predicted[2][2] - predicted[0][2] * predicted[0][2]
        c12 = predicted[0][1] * predicted[0][2] - predicted[0][0] * predicted[1][2]
        c22 = predicted[0][0] * predicted[1][1] - predicted[0][1] * predicted[0][1]
        inverse_det = 1.0 / (predicted[0][0] * c00 + predicted[0][1] * c01 + predicted[0][2] * c02)
        cofactors = unpack([c00, c01, c02, c11, c12, c22])
        for row in range(3):
            scaled = [moved[within][row] * inverse_det for within in range(3)]
            for column in range(3):
                smoother_ref[hour - 1, row, column] = (
                    scaled[0] * cofactors[0][column]
                    + scaled[1] * cofactors[1][column]
                    + scaled[2] * cofactors[2][column]
                )
        return tuple(update(predicted, hour))

    first = tuple(update(stationary, 0))
    lax.fori_loop(1, hours, step, first)


def smoother_kernel(
    times,
    bands,
    slots_used,
    observed_hbm,
    noise_hbm,
    variance_hbm,
    scale_hbm,
    forward_lat_hbm,
    inverse_lat_hbm,
    high_hbm,
    low_hbm,
    out_ref,
    observed_ref,
    noise_ref,
    variance_ref,
    scale_ref,
    forward_lat_ref,
    inverse_lat_ref,
    high,
    low,
    folded,
    outbox,
    inbox,
    outbox_back,
    inbox_back,
    transition_ref,
    gain_ref,
    smoother_ref,
    input_sem,
    table_sem,
    send_sem,
    recv_sem,
    send_back_sem,
    recv_back_sem,
):
    devices = times * bands
    stride = 5 if devices % 5 else 1
    my_time = lax.axis_index("tm")
    my_band = lax.axis_index("space")
    me = my_time * bands + my_band
    lat_dev, lon_size = observed_ref.shape[0], observed_ref.shape[2]
    half = lon_size // 2
    hours = gain_ref.shape[0]
    n_half = gain_ref.shape[2]
    width = LANES // 2

    def table_copy(time, which):
        source, target = ((high_hbm, high), (low_hbm, low))[which]
        return pltpu.make_async_copy(
            source.at[time], target.at[time, :, pl.ds(0, slots_used), :], table_sem.at[time, which]
        )

    inputs = [
        pltpu.make_async_copy(source, target, input_sem.at[index])
        for index, (source, target) in enumerate(
            [
                (observed_hbm, observed_ref),
                (noise_hbm, noise_ref),
                (variance_hbm, variance_ref),
                (scale_hbm, scale_ref),
                (forward_lat_hbm, forward_lat_ref),
                (inverse_lat_hbm, inverse_lat_ref),
            ]
        )
    ]
    inputs[0].start()
    for time in range(times):
        table_copy(time, 0).start()
        table_copy(time, 1).start()
    for copy in inputs[1:]:
        copy.start()

    inbox[...] = jnp.zeros_like(inbox)
    inbox_back[...] = jnp.zeros_like(inbox_back)

    barrier = pltpu.get_barrier_semaphore()

    def greet(step, carry):
        peer = lax.rem(me + step, devices)
        pl.semaphore_signal(
            barrier, inc=1, device_id=(peer // bands, lax.rem(peer, bands)), device_id_type=MESH
        )
        return carry

    lax.fori_loop(1, devices, greet, 0)

    spare = width - slots_used
    high[:, :, slots_used:, :] = jnp.zeros((times, bands, spare, high.shape[3]), high.dtype)
    low[:, :, slots_used:, :] = jnp.zeros((times, bands, spare, low.shape[3]), low.dtype)
    folded[...] = jnp.zeros_like(folded)
    inputs[0].wait()
    for hour in range(2):
        early = observed_ref[:, hour, :half]
        late = observed_ref[:, hour, half:]
        folded[0, hour * ROWS : hour * ROWS + lat_dev, :half] = early + late
        folded[1, hour * ROWS : hour * ROWS + lat_dev, :half] = early - late
    rows = []
    for parity in range(2):
        upper, lower = split(folded[parity])
        rows.append((jnp.concatenate([upper, lower], axis=0), upper))

    def flat(ref, time):
        return ref[time].reshape(bands * width, ref.shape[3])

    for time in range(times):
        table_copy(time, 0).wait()
        table_copy(time, 1).wait()
        both, upper = rows[time % 2]
        wide = lax.dot_general(both, flat(high, time), NT, preferred_element_type=jnp.float32)
        rest = lax.dot_general(upper, flat(low, time), NT, preferred_element_type=jnp.float32)
        spectra = wide[: 2 * ROWS] + wide[2 * ROWS :] + rest
        for pair in range(bands // 2):
            block = spectra[:, pair * LANES : (pair + 1) * LANES]
            owner = time * bands + 2 * pair
            outbox[owner], outbox[owner + 1] = swap_halves(block[:ROWS], block[ROWS:])

    pl.semaphore_wait(barrier, devices - 1)

    def exchange(box, landing, sends, recvs, peer, slot):
        return pltpu.make_async_remote_copy(
            src_ref=box.at[peer, pl.ds(0, lat_dev)],
            dst_ref=landing.at[slot, pl.ds(0, lat_dev)],
            send_sem=sends.at[0],
            recv_sem=recvs.at[slot // bands],
            device_id=(peer // bands, lax.rem(peer, bands)),
            device_id_type=MESH,
        )

    def send(step, carry):
        peer = lax.rem(me + step * stride, devices)
        exchange(outbox, inbox, send_sem, recv_sem, peer, me).start()
        return carry

    def sent(box, sends):
        gone = box.at[pl.ds(0, devices - 1), pl.ds(0, lat_dev)]
        pltpu.make_async_copy(gone, gone, sends.at[0]).wait()

    def arrive(landing, recvs, step):
        time = lax.rem(my_time + step, times)
        come = landing.at[pl.ds(0, bands - 1 if step == 0 else bands), pl.ds(0, lat_dev)]
        pltpu.make_async_copy(come, come, recvs.at[time]).wait()
        return time

    lax.fori_loop(1, devices, send, 0)
    inbox[me] = outbox[me]

    for copy in inputs[1:]:
        copy.wait()
    modes_dev = variance_ref.shape[1]
    slots = modes_dev // times
    mode = lax.broadcasted_iota(jnp.int32, (modes_dev, LANES), 0)
    slot = lax.rem(lax.broadcasted_iota(jnp.int32, (modes_dev, LANES), 1), width)
    picked = ((mode == slot * times + my_time) & (slot < slots)).astype(jnp.float32)
    tile_lane = lax.broadcasted_iota(jnp.int32, (n_half, LANES), 1)

    def own_modes(ref):
        mine = lax.dot_general(ref[...], picked, NN, precision=HIGHEST, preferred_element_type=jnp.float32)
        mine = jnp.where(tile_lane < width, mine[:n_half], mine[n_half:])
        return jnp.where(lax.rem(tile_lane, width) < slots, mine, 1.0)

    symmetric_gains(
        noise_ref, own_modes(variance_ref), own_modes(scale_ref), transition_ref, gain_ref, smoother_ref
    )
    for step in range(times):
        arrive(inbox, recv_sem, step)

    spectra = []
    for time in range(times):
        arrived = inbox[time * bands : (time + 1) * bands].reshape(bands * ROWS, LANES)
        mixed = paired_dot(forward_lat_ref[...], arrived)
        spectra.extend(swap_halves(mixed[:n_half], mixed[n_half:]))

    transition = [[transition_ref[row, column] for column in range(3)] for row in range(3)]
    means, predictions = [], [None]
    means.append([gain_ref[0, row] * spectra[0] for row in range(3)])
    for hour in range(1, hours):
        predicted = mat_vec(transition, means[-1])
        residual = spectra[hour] - predicted[0]
        predictions.append(predicted)
        means.append([predicted[row] + gain_ref[hour, row] * residual for row in range(3)])
    smoothed = means[-1]
    series = [None] * hours
    series[hours - 1] = smoothed[0]
    for hour in range(hours - 2, -1, -1):
        difference = [smoothed[row] - predictions[hour + 1][row] for row in range(3)]
        smoothed = [
            means[hour][row]
            + smoother_ref[hour, row, 0] * difference[0]
            + smoother_ref[hour, row, 1] * difference[1]
            + smoother_ref[hour, row, 2] * difference[2]
            for row in range(3)
        ]
        series[hour] = smoothed[0]

    for time in range(times):
        stacked = jnp.concatenate(swap_halves(series[2 * time], series[2 * time + 1]), axis=0)
        grid = paired_dot(inverse_lat_ref[...], stacked)
        outbox_back[time * bands : (time + 1) * bands] = grid.reshape(bands, ROWS, LANES)

    def send_back(step, carry):
        peer = lax.rem(me + step * stride, devices)
        exchange(outbox_back, inbox_back, send_back_sem, recv_back_sem, peer, me).start()
        return carry

    lax.fori_loop(1, devices, send_back, 0)
    inbox_back[me] = outbox_back[me]

    early = late = 0.0
    for step in range(times):
        time = arrive(inbox_back, recv_back_sem, step)
        blocks = []
        for pair in range(bands // 2):
            owner = time * bands + 2 * pair
            first, second = swap_halves(inbox_back[owner], inbox_back[owner + 1])
            blocks.append(jnp.concatenate([first, second], axis=0))
        upper, lower = split(jnp.concatenate(blocks, axis=1))
        both = jnp.concatenate([upper, lower], axis=0)
        wide = lax.dot_general(both, flat(high, time), NN, preferred_element_type=jnp.float32)
        rest = lax.dot_general(upper, flat(low, time), NN, preferred_element_type=jnp.float32)
        part = wide[: 2 * ROWS] + wide[2 * ROWS :] + rest
        early = early + part
        late = late + jnp.where(lax.rem(time, 2) == 0, part, -part)
    sent(outbox, send_sem)
    sent(outbox_back, send_back_sem)
    for hour in range(2):
        out_ref[:, hour, :half] = early[hour * ROWS : hour * ROWS + lat_dev, :half]
        out_ref[:, hour, half:] = late[hour * ROWS : hour * ROWS + lat_dev, :half]


def per_device_fused(observed, noise_var, spectral_var, time_scale):
    times, bands = lax.axis_size("tm"), lax.axis_size("space")
    hours_dev, lat_dev, lon_size = observed.shape
    hours, lat_size = noise_var.shape[0], spectral_var.shape[1]
    slots_used = round_up(spectral_var.shape[0] // times, 2 * ROWS)
    n_half, width = lat_size // 2, LANES // 2
    half_padded = round_up(lon_size // 2, LANES)

    high, low = lon_tables(lon_size, times, bands, slots_used)
    forward_lat, inverse_lat = lat_tables(lat_size, bands)
    in_vmem = pl.BlockSpec(memory_space=pltpu.VMEM)
    in_place = pl.BlockSpec(memory_space=pltpu.HBM)
    box = pltpu.VMEM((times * bands, ROWS, LANES), jnp.float32)
    table = pltpu.VMEM((times, bands, width, half_padded), jnp.bfloat16)
    dma = pltpu.SemaphoreType.DMA
    field = pl.pallas_call(
        functools.partial(smoother_kernel, times, bands, slots_used),
        out_shape=pltpu.VMEM((lat_dev, hours_dev, lon_size), jnp.float32),
        in_specs=[in_place] * 8,
        out_specs=in_vmem,
        scratch_shapes=[
            pltpu.VMEM((lat_dev, hours_dev, lon_size), jnp.float32),
            pltpu.SMEM((hours,), jnp.float32),
            pltpu.VMEM((lat_size, spectral_var.shape[0]), jnp.float32),
            pltpu.VMEM((lat_size, spectral_var.shape[0]), jnp.float32),
            pltpu.VMEM(forward_lat.shape, jnp.bfloat16),
            pltpu.VMEM(inverse_lat.shape, jnp.bfloat16),
            table,
            table,
            pltpu.VMEM((2, 2 * ROWS, half_padded), jnp.float32),
            box,
            box,
            box,
            box,
            pltpu.VMEM((3, 3, n_half, LANES), jnp.float32),
            pltpu.VMEM((hours, 3, n_half, LANES), jnp.float32),
            pltpu.VMEM((hours, 3, 3, n_half, LANES), jnp.float32),
            dma((6,)),
            dma((times, 2)),
            dma((1,)),
            dma((times,)),
            dma((1,)),
            dma((times,)),
        ],
        compiler_params=pltpu.CompilerParams(collective_id=0, has_side_effects=True),
    )(
        observed.transpose(1, 0, 2),
        noise_var,
        spectral_var.T,
        time_scale.T,
        jnp.asarray(forward_lat),
        jnp.asarray(inverse_lat),
        jnp.asarray(high),
        jnp.asarray(low),
    )
    return field.transpose(1, 0, 2)


def fits(observed, spectral_var):
    times, bands = lax.axis_size("tm"), lax.axis_size("space")
    hours_dev, lat_dev, lon_size = observed.shape
    modes_dev, lat_size = spectral_var.shape
    return (
        hours_dev == 2
        and lat_dev <= ROWS
        and lat_size % (2 * ROWS) == 0
        and bands % 2 == 0
        and times % 2 == 0
        and lon_size % 4 == 0
        and modes_dev % 2 == 0
        and modes_dev % times == 0
        and LANES // 4 < modes_dev // times <= LANES // 2
    )


def per_device(observed, noise_var, spectral_var, time_scale):
    if fits(observed, spectral_var):
        return per_device_fused(observed, noise_var, spectral_var, time_scale)
    return per_device_general(observed, noise_var, spectral_var, time_scale)


def solution(mesh):
    placed = (P("tm", "space", None), P(), P("space", None), P("space", None))
    return jax.shard_map(
        per_device, mesh=mesh, in_specs=placed, out_specs=P("tm", "space", None), check_vma=False
    )
```
